256 devices in a mesh: row: 16 (over y, z_lo, core), col: 16 (over x, z_hi).
Axes of the slice: x: 4, y: 4, z: 8 (z_hi: 4, z_lo: 2; z = z_hi * 2 + z_lo), core: 2. Of those that a mesh axis runs over, the one named last changes fastest.
Arguments:
- support_views: float32 [256, 4, 3, 1024], P(('row', 'col')), may hold values from -6 to 6
- support_pick: int32 [256], P(('row', 'col')), may hold values from 0 to 3
- target_views: float32 [256, 4, 3, 1024], P(('row', 'col')), may hold values from -6 to 6
- target_pick: int32 [256], P(('row', 'col')), may hold values from 0 to 3
- support_labels: float32 [256, 10], P(('row', 'col')), may hold values from -6 to 6
- target_labels: int32 [256], replicated, may hold values from 0 to 9
Outputs:
- support_grad: float32 [256, 3, 1024], P(('row', 'col'))
- label_grad: float32 [256, 10], P(('row', 'col'))
- loss: float32 [], replicated
The draws below stay inside these ranges and needn't reach their ends.
All inputs are finite; a program needn't handle non-finite values.
Results may differ from the reference program's by a relative error of at most 0.00055.
Values sent between devices are 32-bit elements; how exact they have to be, the bound alone decides.
A program may use at most 64 MiB of HBM per device.

```python
import jax
import jax.numpy as jnp
from jax import lax

SIDE = 32
PIX = 1024
CHANNELS = 3
LAYERS = 3
CLASSES = 10
VIEWS = 4
SUPPORT = 256
TARGETS = 256


def set_ends(array, key, least, largest):
    index_at = [jax.random.randint(jax.random.fold_in(key, axis), (), 0, length) for axis, length in enumerate(array.shape)]
    longest = array.shape.index(max(array.shape))
    beside = index_at[:longest] + [(index_at[longest] + 1) % array.shape[longest]] + index_at[longest + 1:]
    return array.at[tuple(index_at)].set(least).at[tuple(beside)].set(largest)


def shard_levels(own_key, shape, cuts, low, largest):
    def one(dim, parts):
        heights = jax.random.uniform(jax.random.fold_in(jax.random.fold_in(own_key, 6), dim), (parts,), jnp.float32, low / len(cuts), largest / len(cuts))
        return jnp.repeat(jnp.exp(heights), shape[dim] // parts).reshape((-1,) + (1,) * (len(shape) - dim - 1))

    gain = one(*cuts[0])
    for cut in cuts[1:]:
        gain = gain * one(*cut)
    return gain


def scatter_about(rng, shape, width, bound, cuts=(), kind=jnp.bfloat16):
    loudness = shard_levels(rng, shape, cuts, -0.22, 0.18) if cuts else 1.0
    array = jax.random.normal(rng, shape, jnp.float32) * width * loudness
    return jnp.minimum(jnp.maximum(array, -bound), bound).astype(kind)


def setup_inputs(seed: int = 0) -> dict:
    keys = jax.random.split(jax.random.key(seed), 7)
    return {
        "support_views": scatter_about(keys[0], (SUPPORT, VIEWS, CHANNELS, PIX), 1.0, 6.0, ((0, 256),), jnp.float32),
        "support_pick": set_ends(jax.random.randint(keys[1], (SUPPORT,), 0, VIEWS), jax.random.fold_in(keys[1], 1), 0, VIEWS - 1).astype(jnp.int32),
        "target_views": scatter_about(keys[2], (TARGETS, VIEWS, CHANNELS, PIX), 1.0, 6.0, ((0, 256),), jnp.float32),
        "target_pick": set_ends(jax.random.randint(keys[3], (TARGETS,), 0, VIEWS), jax.random.fold_in(keys[3], 1), 0, VIEWS - 1).astype(jnp.int32),
        "support_labels": scatter_about(keys[4], (SUPPORT, CLASSES), 1.0, 6.0, ((0, 256),), jnp.float32),
        "target_labels": set_ends(jax.random.randint(keys[5], (TARGETS,), 0, CLASSES), jax.random.fold_in(keys[5], 1), 0, CLASSES - 1).astype(jnp.int32),
    }


bias_variance = 0.1
ridge_scale = 0.1
highest = lax.Precision.HIGHEST

def shifted(surface, offset):
    extent = surface.shape[-1]
    padding = jnp.zeros(surface.shape[:-1] + (abs(offset),), surface.dtype)
    if offset > 0:
        return jnp.concatenate([surface[..., offset:], padding], axis=-1)
    return jnp.concatenate([padding, surface[..., :extent + offset]], axis=-1)

def average(surface):
    column = jnp.arange(surface.shape[-1], dtype=jnp.int32) % SIDE
    rightward = jnp.where(column < SIDE - 1, shifted(surface, 1), 0.0)
    leftward = jnp.where(column > 0, shifted(surface, -1), 0.0)
    across = surface + leftward + rightward
    return (across + shifted(across, SIDE) + shifted(across, -SIDE)) / 9.0

def choose_view(views, picked):
    options = jnp.arange(views.shape[1], dtype=jnp.int32)
    selector = (picked[:, None] == options[None, :]).astype(jnp.float32)
    return lax.optimization_barrier(jnp.sum(selector[:, :, None, None] * views, axis=1))

def self_maps(images):
    energy = lax.optimization_barrier(jnp.sum(images * images, axis=1)) / images.shape[1]
    current = average(energy) + bias_variance
    stacked = [current]
    for layer in range(1, LAYERS):
        current = average(current) + bias_variance
        stacked.append(current)
    return jnp.stack(stacked, axis=1)

def self_back(images, grad_maps):
    carry = grad_maps[:, -1]
    for layer in range(grad_maps.shape[1] - 2, -1, -1):
        carry = grad_maps[:, layer] + average(carry)
    return average(carry)[:, None, :] * images * (2.0 / images.shape[1])

def arc(kernel_map, first_diag, second_diag):
    scale_map = jnp.sqrt(first_diag * second_diag)
    cosine = jnp.clip(kernel_map / scale_map, -1.0, 1.0)
    sine = jnp.sqrt(1.0 - cosine * cosine)
    angle = jnp.arccos(cosine)
    value = scale_map * (sine + (jnp.pi - angle) * cosine) / jnp.pi
    slope = (jnp.pi - angle) / jnp.pi
    spread = scale_map * sine / (2.0 * jnp.pi)
    return (value, slope, spread)

def pair_forward(first, first_maps, second, second_maps):
    product = first[:, None, 0] * second[None, :, 0]
    for channel in range(1, first.shape[1]):
        product = product + first[:, None, channel] * second[None, :, channel]
    current = average(product / first.shape[1]) + bias_variance
    slopes = []
    spreads = []
    depth = first_maps.shape[1]
    for layer in range(depth):
        value, slope, spread = arc(current, first_maps[:, None, layer], second_maps[None, :, layer])
        slopes.append(slope)
        spreads.append(spread)
        if layer + 1 < depth:
            current = average(value) + bias_variance
    return (lax.optimization_barrier(jnp.mean(value, axis=-1)), slopes, spreads)

def pair_backward(first, first_maps, second, second_maps, weights, want_second):
    kernel, slopes, spreads = pair_forward(first, first_maps, second, second_maps)
    depth = first_maps.shape[1]
    grad = jnp.broadcast_to(weights[:, :, None] / first.shape[-1], slopes[0].shape)
    first_parts = []
    second_parts = []
    for layer in range(depth - 1, -1, -1):
        scaled = grad * spreads[layer]
        first_parts.insert(0, lax.optimization_barrier(jnp.sum(scaled, axis=1)) / first_maps[:, layer])
        if want_second:
            second_parts.insert(0, lax.optimization_barrier(jnp.sum(scaled, axis=0)) / second_maps[:, layer])
        grad = average(grad * slopes[layer])
    first_image = jnp.stack([lax.optimization_barrier(jnp.sum(grad * second[None, :, channel], axis=1)) for channel in range(first.shape[1])], axis=1) / first.shape[1]
    if not want_second:
        return (first_image, jnp.stack(first_parts, axis=1), None, None)
    second_image = jnp.stack([lax.optimization_barrier(jnp.sum(grad * first[:, None, channel], axis=0)) for channel in range(first.shape[1])], axis=1) / first.shape[1]
    return (first_image, jnp.stack(first_parts, axis=1), second_image, jnp.stack(second_parts, axis=1))

def solve_with(factor, rhs):
    halfway = lax.linalg.triangular_solve(factor, rhs, left_side=True, lower=True)
    return lax.linalg.triangular_solve(factor, halfway, left_side=True, lower=True, transpose_a=True)

def reference(support_views, support_pick, target_views, target_pick, support_labels, target_labels):
    support = choose_view(support_views, support_pick)
    targets = choose_view(target_views, target_pick)
    support_maps = self_maps(support)
    target_maps = self_maps(targets)
    block_rows = 8
    block_count = SUPPORT // block_rows
    support_blocks = support.reshape(block_count, block_rows, CHANNELS, PIX)
    map_blocks = support_maps.reshape(block_count, block_rows, LAYERS, PIX)

    def forward_block(inputs):
        block, block_maps = inputs
        inner, _, _ = pair_forward(block, block_maps, support, support_maps)
        outer, _, _ = pair_forward(block, block_maps, targets, target_maps)
        return (inner, outer)
    inner, outer = lax.map(forward_block, (support_blocks, map_blocks))
    support_kernel = inner.reshape(SUPPORT, SUPPORT)
    cross_kernel = outer.reshape(SUPPORT, TARGETS)
    identity = jnp.eye(SUPPORT, dtype=jnp.float32)
    trace_mean = jnp.trace(support_kernel) / SUPPORT
    system = support_kernel + ridge_scale * trace_mean * identity
    factor = jnp.linalg.cholesky(system)
    alpha = solve_with(factor, support_labels)
    onehot = (target_labels[:, None] == jnp.arange(CLASSES, dtype=jnp.int32)[None, :]).astype(jnp.float32) - 1.0 / CLASSES
    predicted = jnp.dot(cross_kernel.T, alpha, precision=highest)
    error = predicted - onehot
    loss = 0.5 * jnp.sum(error * error)
    adjoint = jnp.dot(cross_kernel, error, precision=highest)
    gamma = solve_with(factor, adjoint)
    intersection = jnp.sum(gamma * alpha)
    cross_weights = jnp.dot(alpha, error.T, precision=highest)
    support_weights = -jnp.dot(gamma, alpha.T, precision=highest) - ridge_scale * intersection / SUPPORT * identity

    def backward_block(carry, inputs):
        block, block_maps, inner_weights, outer_weights = inputs
        grad_one, maps_one, grad_two, maps_two = pair_backward(block, block_maps, support, support_maps, inner_weights, True)
        grad_three, maps_three, _, _ = pair_backward(block, block_maps, targets, target_maps, outer_weights, False)
        column_images, column_maps = carry
        return ((column_images + grad_two, column_maps + maps_two), (grad_one + grad_three, maps_one + maps_three))
    start = (jnp.zeros((SUPPORT, CHANNELS, PIX), jnp.float32), jnp.zeros((SUPPORT, LAYERS, PIX), jnp.float32))
    (column_images, column_maps), (row_images, row_maps) = lax.scan(backward_block, start, (support_blocks, map_blocks, support_weights.reshape(block_count, block_rows, SUPPORT), cross_weights.reshape(block_count, block_rows, TARGETS)))
    image_grad = row_images.reshape(SUPPORT, CHANNELS, PIX) + column_images
    map_grad = row_maps.reshape(SUPPORT, LAYERS, PIX) + column_maps
    support_grad = image_grad + self_back(support, map_grad)
    return (support_grad, gamma, loss)
```

```python
import jax
import jax.numpy as jnp
import numpy as np
from jax import lax
from jax.experimental import pallas as pl
from jax.experimental.pallas import tpu as pltpu
from jax.sharding import PartitionSpec as P

PI = float(np.pi)
BIAS = 0.1
RIDGE = 0.1
GROUP = 16
PIX = 1024
SUPPORT = 256
CLASSES = 10
HIGHEST = lax.Precision.HIGHEST
F32 = jnp.float32
BF16 = jnp.bfloat16
ACOS = (
    1.570796251296997,
    -0.21459108591079712,
    0.08883588761091232,
    -0.04919743537902832,
    0.027762912213802338,
    -0.012003393843770027,
    0.0026117200031876564,
)


def inverse_schedule():
    low, high = RIDGE * 0.99, SUPPORT + 2 * RIDGE
    first = 2.0 / (low + high)
    error = (high - low) / (high + low)
    scales = []
    while error > 1e-7:
        scales.append(2.0 / (2.0 - error * error))
        error = error * error / (2.0 - error * error)
    return first, scales


FIRST_SCALE, SCALES = inverse_schedule()


def make_masks():
    lane = lax.broadcasted_iota(jnp.int32, (8, 128), 1)
    sub = lax.broadcasted_iota(jnp.int32, (8, 128), 0)
    col = lane & 31
    return dict(
        right=(col < 31).astype(F32),
        left=(col > 0).astype(F32),
        below=(sub < 7).astype(F32),
        above=(sub > 0).astype(F32),
        group=lane // 32,
        lane=lane,
    )


def box(x, m):
    h = (
        x
        + m["right"] * pltpu.roll(x, 127, x.ndim - 1)
        + m["left"] * pltpu.roll(x, 1, x.ndim - 1)
    )
    h0, h1, h2, h3 = (h[..., k, :, :] for k in range(4))
    above = pltpu.roll(h3, 1, h3.ndim - 2) * m["above"]
    below = pltpu.roll(h0, 7, h3.ndim - 2) * m["below"]
    a = h0 + h1
    b = h2 + h3
    return jnp.stack([above + a, a + h2, h1 + b, b + below], axis=-3)


def arc(c):
    c = jnp.clip(c, -1.0, 1.0)
    t = jnp.abs(c)
    w = 1.0 - t
    v = 1.0 + t
    q = w * lax.rsqrt(jnp.maximum(w, 1e-30))
    s = q * (v * lax.rsqrt(v))
    p = jnp.full_like(t, ACOS[-1])
    for a in ACOS[-2::-1]:
        p = p * t + a
    theta = q * p
    return s, jnp.where(c < 0, theta, PI - theta), c


def repeat_lanes(x, m):
    rolled = [x] + [pltpu.roll(x, 32 * i, x.ndim - 1) for i in (1, 2, 3)]
    out = []
    for k in range(4):
        y = rolled[0]
        for i in (1, 2, 3):
            y = jnp.where(m["group"] == ((k + i) % 4), rolled[i], y)
        out.append(y)
    return jnp.stack(out, axis=-3)


def pack_lanes(maps, m):
    rolled = [[x if i == 0 else pltpu.roll(x, 32 * i, x.ndim - 1) for i in range(4)] for x in maps]
    out = []
    for k in range(4):
        y = rolled[0][(0 - k) % 4]
        for j in (1, 2, 3):
            y = jnp.where(m["group"] == j, rolled[j][(j - k) % 4], y)
        out.append(y)
    return jnp.stack(out, axis=-3)


def merge_lanes(x, m):
    last = x.ndim - 1
    x = x + pltpu.roll(x, 64, last)
    x = x + pltpu.roll(x, 32, last)
    y = x[..., 0, :, :]
    for k in (1, 2, 3):
        y = jnp.where(m["group"] == k, x[..., k, :, :], y)
    return y


def self_maps(x, m):
    d = box((x[:, 0] * x[:, 0] + x[:, 1] * x[:, 1] + x[:, 2] * x[:, 2]) * (1.0 / 27.0), m) + BIAS
    maps = [d]
    for _ in range(2):
        d = box(d, m) * (1.0 / 9.0) + BIAS
        maps.append(d)
    return maps


def dot3(a, b):
    ah = a.astype(BF16)
    al = (a - ah.astype(F32)).astype(BF16)
    bh = b.astype(BF16)
    bl = (b - bh.astype(F32)).astype(BF16)
    d = lambda p, q: jnp.dot(p, q, preferred_element_type=F32)
    return d(ah, bh) + (d(ah, bl) + d(al, bh))


def dot6(a, b):
    return jnp.dot(a, b, precision=HIGHEST, preferred_element_type=F32)


def dot_nt(a, b):
    return lax.dot_general(
        a, b, (((1,), (1,)), ((), ())), precision=HIGHEST, preferred_element_type=F32
    )


def invert(a, identity):
    x = (SCALES[0] * FIRST_SCALE) * (2.0 * identity - FIRST_SCALE * a)
    count = len(SCALES)
    for i in range(1, count):
        mul = dot6 if i >= count - 2 else dot3
        x = SCALES[i] * mul(x, 2.0 * identity - mul(a, x))
    return x


def step_kernel(
    views_ref,
    pick_ref,
    target_views_ref,
    target_pick_ref,
    labels_ref,
    classes_ref,
    grad_out,
    label_out,
    loss_out,
    own,
    vraw,
    uraw,
    ui,
    um,
    vi,
    vm,
    phis,
    sines,
    partial,
    tile1,
    send_a,
    send_b,
    abuf,
    bbuf,
    side1,
    side2,
    wbuf,
    gsend,
    grecv,
    img_row_s,
    img_row_r,
    img_col_s,
    img_col_r,
    t1_s,
    t1_r,
    t2a_s,
    t2a_r,
    t2b_s,
    t2b_r,
    fin_s,
    fin_r,
):
    row = lax.axis_index("row")
    col = lax.axis_index("col")
    m = make_masks()

    def row_peer(d):
        return lax.rem(row + d, GROUP)

    def col_peer(d):
        return lax.rem(col + d, GROUP)

    def each_peer(body):
        def step(d, carry):
            body(d)
            return carry

        lax.fori_loop(1, GROUP, step, 0)

    def remote(src, dst, ssem, rsem, axis, peer):
        other = {"row": (peer, col), "col": (row, peer)}[axis]
        return pltpu.make_async_remote_copy(
            src_ref=src,
            dst_ref=dst,
            send_sem=ssem,
            recv_sem=rsem,
            device_id=other,
            device_id_type=pl.DeviceIdType.MESH,
        )

    def image_row(d, me, peer):
        return remote(own, vraw.at[me], img_row_s.at[d], img_row_r.at[me], "row", peer)

    def image_col(d, me, peer):
        return remote(own.at[pl.ds(0, 3)], uraw.at[me], img_col_s.at[d], img_col_r.at[me], "col", peer)

    def tile_row(d, me, peer):
        return remote(tile1.at[row], tile1.at[me], t1_s.at[d], t1_r.at[me], "row", peer)

    def block_a(d, me, peer):
        return remote(send_a, abuf.at[:, pl.ds(me * GROUP, GROUP)], t2a_s.at[d], t2a_r.at[me], "col", peer)

    def block_b(d, me, peer):
        return remote(send_b, bbuf.at[:, pl.ds(me * GROUP, GROUP)], t2b_s.at[d], t2b_r.at[me], "col", peer)

    def grad_col(d, me, peer):
        return remote(gsend.at[peer], grecv.at[me], fin_s.at[d], fin_r.at[me], "col", peer)

    def start_row(copy):
        each_peer(lambda d: copy(d, row, row_peer(d)).start())

    def start_col(copy):
        each_peer(lambda d: copy(d, col, col_peer(d)).start())

    def landed_row(copy):
        each_peer(lambda d: copy(d, row_peer(d), row_peer(d)).wait_recv())

    def landed_col(copy):
        each_peer(lambda d: copy(d, col_peer(d), col_peer(d)).wait_recv())

    barrier = pltpu.get_barrier_semaphore()

    def greet(d):
        pl.semaphore_signal(
            barrier, inc=1, device_id=(row_peer(d), col), device_id_type=pl.DeviceIdType.MESH
        )
        pl.semaphore_signal(
            barrier, inc=1, device_id=(row, col_peer(d)), device_id_type=pl.DeviceIdType.MESH
        )

    each_peer(greet)

    support = views_ref[0, pick_ref[0]]
    target = target_views_ref[0, target_pick_ref[0]]
    for k in range(8):
        own[0:3, k, :] = support[:, k * 128 : (k + 1) * 128]
        own[3:6, k, :] = target[:, k * 128 : (k + 1) * 128]
    own[6] = jnp.zeros((8, 128), F32)
    own[6, 0:1, 0:CLASSES] = labels_ref[...]
    pl.semaphore_wait(barrier, 2 * (GROUP - 1))
    start_row(image_row)
    start_col(image_col)
    vraw[row] = own[...]
    uraw[col] = own[0:3]
    landed_col(image_col)

    def prepare_rows(i, carry):
        us = pl.ds(i * 4, 4)
        x = repeat_lanes(uraw[us], m)
        ui[us] = x
        for l, d in enumerate(self_maps(x, m)):
            r = lax.rsqrt(d)
            um[us, l] = d * r * (1.0 / (9.0 * PI) if l < 2 else 1.0)
            um[us, 3 + l] = r
        return carry

    lax.fori_loop(0, 4, prepare_rows, 0)
    landed_row(image_row)
    for h in range(2):
        vs = pl.ds(4 * h, 4)
        x = pack_lanes(
            [vraw[pl.ds(8 * (j % 2) + 4 * h, 4), 3 * (j // 2) : 3 * (j // 2) + 3] for j in range(4)], m
        )
        vi[vs] = x * (1.0 / 27.0)
        for l, d in enumerate(self_maps(x, m)):
            r = lax.rsqrt(d)
            vm[vs, l] = d * r
            vm[vs, 3 + l] = r

    def forward(u, carry):
        k = box(ui[u, 0] * vi[:, 0] + ui[u, 1] * vi[:, 1] + ui[u, 2] * vi[:, 2], m) + BIAS
        for l in range(3):
            s, phi, c = arc(k * (um[u, 3 + l] * vm[:, 3 + l]))
            z = (s + phi * c) * (um[u, l] * vm[:, l])
            phis[l, u] = phi
            sines[l, u] = s * vm[:, l]
            if l < 2:
                k = box(z, m) + BIAS
        partial[u] = jnp.sum(jnp.sum(z, axis=1), axis=1)
        return carry

    lax.fori_loop(0, GROUP, forward, 0, unroll=2)

    shift = lax.rem(row, 8) * GROUP
    for j in range(4):
        acc = jnp.zeros((8, 128), F32)
        for u in range(GROUP):
            total = jnp.sum(jnp.where(m["group"] == j, partial[u], 0.0), axis=1, keepdims=True)
            acc = jnp.where(m["lane"] == shift + u, total, acc)
        tile1[row, 8 * j : 8 * j + 8] = acc * (1.0 / (PIX * PI))
    start_row(tile_row)

    def backward(u, carry):
        g = box(phis[2, u], m)
        sines[1, u] = g * sines[1, u]
        g = box(g * phis[1, u], m)
        sines[0, u] = g * sines[0, u]
        phis[0, u] = box(g * phis[0, u], m)
        return carry

    lax.fori_loop(0, 6, backward, 0, unroll=2)
    landed_row(tile_row)
    low = tile1[0]
    high = tile1[8]
    for i in range(1, 8):
        low = low + tile1[i]
        high = high + tile1[8 + i]
    send_a[0] = low[0:16]
    send_a[1] = high[0:16]
    send_b[0] = low[16:32]
    send_b[1] = high[16:32]
    for i in range(GROUP):
        send_a[2, i : i + 1, :] = vraw[i, 6, 0:1, :]
    start_col(block_a)
    start_col(block_b)
    abuf[:, pl.ds(col * GROUP, GROUP)] = send_a[...]
    bbuf[:, pl.ds(col * GROUP, GROUP)] = send_b[...]
    lax.fori_loop(6, GROUP, backward, 0, unroll=2)
    landed_col(block_a)

    natural = lambda ref, part: jnp.concatenate(
        [ref[part, pl.ds(i, GROUP, stride=GROUP), :] for i in range(GROUP)], axis=0
    )
    kss = jnp.concatenate([natural(abuf, 0), natural(abuf, 1)], axis=1)
    labels_t = jnp.transpose(natural(abuf, 2))[0:16]
    rows = lax.broadcasted_iota(jnp.int32, (256, 256), 0)
    cols = lax.broadcasted_iota(jnp.int32, (256, 256), 1)
    identity = (rows == cols).astype(F32)
    trace = jnp.sum(jnp.sum(kss * identity, axis=0, keepdims=True), axis=1, keepdims=True) * (
        1.0 / SUPPORT
    )
    scale = 1.0 / trace
    system = kss * scale + RIDGE * identity
    inverse = invert(system, identity)

    def solve(rhs_t):
        first = dot6(rhs_t, inverse)
        return (first + dot6(rhs_t - dot6(first, system), inverse)) * scale

    alpha_t = solve(labels_t)
    landed_col(block_b)
    kst_t = jnp.concatenate([natural(bbuf, 0), natural(bbuf, 1)], axis=1)
    class_row = lax.broadcasted_iota(jnp.int32, (16, 256), 0)
    wanted = jnp.where(
        class_row < CLASSES,
        (classes_ref[...] == class_row).astype(F32) - 1.0 / CLASSES,
        0.0,
    )
    error_t = dot_nt(alpha_t, kst_t) - wanted
    loss = jnp.sum(jnp.sum(error_t * error_t, axis=0, keepdims=True), axis=1, keepdims=True)
    loss_out[...] = 0.5 * loss
    gamma_t = solve(dot6(error_t, kst_t))
    inner = jnp.sum(jnp.sum(gamma_t * alpha_t, axis=0, keepdims=True), axis=1, keepdims=True)

    pad = jnp.zeros((80, 256), F32)
    side1[...] = jnp.transpose(jnp.concatenate([alpha_t, gamma_t, error_t, pad], axis=0))
    side2[...] = jnp.transpose(jnp.concatenate([-gamma_t, -alpha_t, alpha_t, pad], axis=0))
    mine = side1[pl.ds(col, GROUP, stride=GROUP), :]
    lane16 = lax.broadcasted_iota(jnp.int32, (16, 128), 1)
    sub16 = lax.broadcasted_iota(jnp.int32, (16, 128), 0)
    left = jnp.concatenate(
        [jnp.where(lane16 < 32, mine, 0.0), jnp.where(lane16 < 32, 0.0, mine)], axis=0
    )
    right = jnp.concatenate(
        [side2[pl.ds(row * GROUP, GROUP), :], jnp.zeros((112, 128), F32)], axis=0
    )
    weights = dot_nt(left, right)
    on_diagonal = ((sub16 == row) & (lane16 == col)).astype(F32)
    weights = jnp.concatenate(
        [weights[0:16] - (2.0 * RIDGE / SUPPORT) * inner * on_diagonal, weights[16:32]], axis=0
    )
    own_row = side1[pl.ds(row * GROUP + col, 1), :]
    label_out[...] = own_row[:, 16 : 16 + CLASSES]
    for u in range(GROUP):
        y = weights[0:8, u : u + 1] * jnp.ones((8, 128), F32)
        for j in (1, 2, 3):
            y = jnp.where(m["group"] == j, weights[8 * j : 8 * j + 8, u : u + 1], y)
        wbuf[u] = y

    step9 = 1.0 / (9.0 * PI)

    def contract(u, carry):
        h1 = h2 = h3 = g0 = g1 = g2 = None
        plus = lambda total, term: term if total is None else total + term
        for v in range(8):
            w = jnp.broadcast_to(wbuf[u, v : v + 1, :], (8, 128))
            h1 = plus(h1, w * sines[0, u, v])
            h2 = plus(h2, w * sines[1, u, v])
            h3 = plus(h3, w * sines[2, u, v])
            g = w * phis[0, u, v]
            g0 = plus(g0, g * vi[v, 0])
            g1 = plus(g1, g * vi[v, 1])
            g2 = plus(g2, g * vi[v, 2])
        each = 1.0 / (2.0 * PI * PIX)
        h3 = h3 * um[u, 5] * each
        h2 = h2 * um[u, 4] * (each * step9)
        h1 = h1 * um[u, 3] * (each * step9 * step9)
        back = h1 + box(h2 + box(h3, m) * (1.0 / 9.0), m) * (1.0 / 9.0)
        back = box(back, m) * (2.0 / 27.0)
        scale_image = 27.0 * step9**3 / (3.0 * PIX)
        x = ui[u]
        out = jnp.stack([g0, g1, g2], axis=0) * scale_image + back * x
        gsend[u] = merge_lanes(out, m)
        return carry

    lax.fori_loop(0, GROUP, contract, 0, unroll=2)
    start_col(grad_col)
    grecv[col] = gsend[col]
    landed_col(grad_col)
    total = grecv[0]
    for i in range(1, GROUP):
        total = total + grecv[i]
    for k in range(8):
        grad_out[0, :, k * 128 : (k + 1) * 128] = total[:, k, :]

    def sent(d):
        image_row(d, row, row_peer(d)).wait_send()
        image_col(d, col, col_peer(d)).wait_send()
        tile_row(d, row, row_peer(d)).wait_send()
        block_a(d, col, col_peer(d)).wait_send()
        block_b(d, col, col_peer(d)).wait_send()
        grad_col(d, col, col_peer(d)).wait_send()

    each_peer(sent)


def body(support_views, support_pick, target_views, target_pick, support_labels, target_labels):
    vmem = pl.BlockSpec(memory_space=pltpu.VMEM)
    smem = pl.BlockSpec(memory_space=pltpu.SMEM)
    buf = lambda *shape: pltpu.VMEM(shape, F32)
    grad, label_grad, loss = pl.pallas_call(
        step_kernel,
        name="kip_step",
        out_shape=(
            jax.ShapeDtypeStruct((1, 3, PIX), F32),
            jax.ShapeDtypeStruct((1, CLASSES), F32),
            jax.ShapeDtypeStruct((1, 1), F32),
        ),
        in_specs=[vmem, smem, vmem, smem, vmem, vmem],
        out_specs=(vmem, vmem, vmem),
        scratch_shapes=[
            buf(7, 8, 128),
            buf(GROUP, 7, 8, 128),
            buf(GROUP, 3, 8, 128),
            buf(GROUP, 3, 4, 8, 128),
            buf(GROUP, 6, 4, 8, 128),
            buf(8, 3, 4, 8, 128),
            buf(8, 6, 4, 8, 128),
            buf(3, GROUP, 8, 4, 8, 128),
            buf(3, GROUP, 8, 4, 8, 128),
            buf(GROUP, 8, 128),
            buf(GROUP, 32, 128),
            buf(3, GROUP, 128),
            buf(2, GROUP, 128),
            buf(3, 256, 128),
            buf(2, 256, 128),
            buf(256, 128),
            buf(256, 128),
            buf(GROUP, 8, 128),
            buf(GROUP, 3, 8, 128),
            buf(GROUP, 3, 8, 128),
        ]
        + [pltpu.SemaphoreType.DMA((GROUP,))] * 12,
        compiler_params=pltpu.CompilerParams(
            collective_id=0, has_side_effects=True, vmem_limit_bytes=56 << 20
        ),
    )(
        support_views,
        support_pick,
        target_views,
        target_pick,
        support_labels,
        target_labels.reshape(1, SUPPORT),
    )
    return grad, label_grad, loss.reshape(())


def solution(mesh):
    both = ("row", "col")
    return jax.shard_map(
        body,
        mesh=mesh,
        in_specs=(
            P(both, None, None, None),
            P(both),
            P(both, None, None, None),
            P(both),
            P(both, None),
            P(),
        ),
        out_specs=(P(both, None, None), P(both, None), P()),
        check_vma=False,
    )
```

```python
import jax
import jax.numpy as jnp
import numpy as np
from jax import lax
from jax.experimental import pallas as pl
from jax.experimental.pallas import tpu as pltpu
from jax.sharding import PartitionSpec as P

PI = float(np.pi)
BIAS = 0.1
RIDGE = 0.1
GROUP = 16
PIX = 1024
SUPPORT = 256
CLASSES = 10
HIGHEST = lax.Precision.HIGHEST
F32 = jnp.float32
BF16 = jnp.bfloat16
ACOS = (
    1.570796251296997,
    -0.21459108591079712,
    0.08883588761091232,
    -0.04919743537902832,
    0.027762912213802338,
    -0.012003393843770027,
    0.0026117200031876564,
)


def inverse_schedule():
    low, high = RIDGE * 0.99, SUPPORT + 2 * RIDGE
    first = 2.0 / (low + high)
    error = (high - low) / (high + low)
    scales = []
    while error > 1e-7:
        scales.append(2.0 / (2.0 - error * error))
        error = error * error / (2.0 - error * error)
    return first, scales


FIRST_SCALE, SCALES = inverse_schedule()


def make_masks():
    lane = lax.broadcasted_iota(jnp.int32, (8, 128), 1)
    sub = lax.broadcasted_iota(jnp.int32, (8, 128), 0)
    col = lane & 31
    return dict(
        right=(col < 31).astype(F32),
        left=(col > 0).astype(F32),
        below=(sub < 7).astype(F32),
        above=(sub > 0).astype(F32),
        group=lane // 32,
        lane=lane,
    )


def box(x, m):
    h = (
        x
        + m["right"] * pltpu.roll(x, 127, x.ndim - 1)
        + m["left"] * pltpu.roll(x, 1, x.ndim - 1)
    )
    h0, h1, h2, h3 = (h[..., k, :, :] for k in range(4))
    above = pltpu.roll(h3, 1, h3.ndim - 2) * m["above"]
    below = pltpu.roll(h0, 7, h3.ndim - 2) * m["below"]
    a = h0 + h1
    b = h2 + h3
    return jnp.stack([above + a, a + h2, h1 + b, b + below], axis=-3)


def arc(c):
    t = jnp.abs(c)
    w = jnp.maximum(1.0 - t, 1e-30)
    v = 1.0 + t
    q = w * lax.rsqrt(w)
    s = q * (v * lax.rsqrt(v))
    p = jnp.full_like(t, ACOS[-1])
    for a in ACOS[-2::-1]:
        p = p * t + a
    theta = q * p
    return s, jnp.where(c < 0, theta, PI - theta)


def repeat_lanes(x, m):
    rolled = [x] + [pltpu.roll(x, 32 * i, x.ndim - 1) for i in (1, 2, 3)]
    out = []
    for k in range(4):
        y = rolled[0]
        for i in (1, 2, 3):
            y = jnp.where(m["group"] == ((k + i) % 4), rolled[i], y)
        out.append(y)
    return jnp.stack(out, axis=-3)


def pack_lanes(maps, m):
    rolled = [[x if i == 0 else pltpu.roll(x, 32 * i, x.ndim - 1) for i in range(4)] for x in maps]
    out = []
    for k in range(4):
        y = rolled[0][(0 - k) % 4]
        for j in (1, 2, 3):
            y = jnp.where(m["group"] == j, rolled[j][(j - k) % 4], y)
        out.append(y)
    return jnp.stack(out, axis=-3)


def merge_lanes(x, m):
    last = x.ndim - 1
    x = x + pltpu.roll(x, 64, last)
    x = x + pltpu.roll(x, 32, last)
    y = x[..., 0, :, :]
    for k in (1, 2, 3):
        y = jnp.where(m["group"] == k, x[..., k, :, :], y)
    return y


def self_maps(x, m):
    d = box((x[:, 0] * x[:, 0] + x[:, 1] * x[:, 1] + x[:, 2] * x[:, 2]) * (1.0 / 27.0), m) + BIAS
    maps = [d]
    for _ in range(2):
        d = box(d, m) * (1.0 / 9.0) + BIAS
        maps.append(d)
    return maps


def dot3(a, b):
    ah = a.astype(BF16)
    al = (a - ah.astype(F32)).astype(BF16)
    bh = b.astype(BF16)
    bl = (b - bh.astype(F32)).astype(BF16)
    d = lambda p, q: jnp.dot(p, q, preferred_element_type=F32)
    return d(ah, bh) + (d(ah, bl) + d(al, bh))


def dot6(a, b):
    return jnp.dot(a, b, precision=HIGHEST, preferred_element_type=F32)


def dot_nt(a, b):
    return lax.dot_general(
        a, b, (((1,), (1,)), ((), ())), precision=HIGHEST, preferred_element_type=F32
    )


def invert(a, identity):
    x = (SCALES[0] * FIRST_SCALE) * (2.0 * identity - FIRST_SCALE * a)
    count = len(SCALES)
    for i in range(1, count):
        mul = dot6 if i >= count - 2 else dot3
        x = SCALES[i] * mul(x, 2.0 * identity - mul(a, x))
    return x


def step_kernel(
    views_ref,
    pick_ref,
    target_views_ref,
    target_pick_ref,
    labels_ref,
    classes_ref,
    grad_out,
    label_out,
    loss_out,
    own,
    vraw,
    uraw,
    ui,
    um,
    vi,
    vm,
    phis,
    sines,
    partial,
    packed,
    send_a,
    send_b,
    abuf,
    bbuf,
    side1,
    side2,
    wbuf,
    gsend,
    grecv,
    img_row_s,
    img_row_r,
    img_col_s,
    img_col_r,
    t1_s,
    t1_r,
    t2a_s,
    t2a_r,
    t2b_s,
    t2b_r,
    fin_s,
    fin_r,
):
    row = lax.axis_index("row")
    col = lax.axis_index("col")
    sibling = row + 1 - 2 * lax.rem(row, 2)
    m = make_masks()

    def row_peer(d):
        return lax.rem(row + d, GROUP)

    def col_peer(d):
        return lax.rem(col + d, GROUP)

    def same_core(d):
        return lax.rem(row + 2 * d, GROUP)

    def along_z(d):
        return (col // 4) * 4 + lax.rem(col + d, 4)

    def along_x(d):
        return lax.rem(col + 4 * d, GROUP)

    def loop(low, high, body):
        def step(d, carry):
            body(d)
            return carry

        lax.fori_loop(low, high, step, 0)

    def remote(src, dst, ssem, rsem, device):
        return pltpu.make_async_remote_copy(
            src_ref=src,
            dst_ref=dst,
            send_sem=ssem,
            recv_sem=rsem,
            device_id=device,
            device_id_type=pl.DeviceIdType.MESH,
        )

    def image_row(src, k, slot, peer):
        return remote(src, vraw.at[slot], img_row_s.at[k], img_row_r.at[slot], (peer, col))

    def image_col(src, k, slot, peer):
        return remote(src, uraw.at[slot], img_col_s.at[k], img_col_r.at[slot], (row, peer))

    def tile_col(d, slot, peer):
        return remote(packed.at[col], packed.at[slot], t1_s.at[d], t1_r.at[slot], (row, peer))

    def block_a(d, slot, peer):
        return remote(
            send_a, abuf.at[:, pl.ds(slot * GROUP, GROUP)], t2a_s.at[d], t2a_r.at[slot], (peer, col)
        )

    def block_b(d, slot, peer):
        return remote(
            send_b, bbuf.at[:, pl.ds(slot * GROUP, GROUP)], t2b_s.at[d], t2b_r.at[slot], (peer, col)
        )

    def grad_col(d, slot, peer):
        return remote(gsend.at[peer], grecv.at[slot], fin_s.at[d], fin_r.at[slot], (row, peer))

    barrier = pltpu.get_barrier_semaphore()

    def greet(d):
        pl.semaphore_signal(
            barrier, inc=1, device_id=(row, col_peer(d)), device_id_type=pl.DeviceIdType.MESH
        )
        pl.semaphore_signal(
            barrier, inc=1, device_id=(row_peer(d), col), device_id_type=pl.DeviceIdType.MESH
        )

    loop(1, GROUP, greet)

    for c in range(3):
        support = views_ref[0, c, pl.ds(pick_ref[0], 1), :]
        target = target_views_ref[0, c, pl.ds(target_pick_ref[0], 1), :]
        for k in range(8):
            own[c, k : k + 1, :] = support[:, k * 128 : (k + 1) * 128]
            own[3 + c, k : k + 1, :] = target[:, k * 128 : (k + 1) * 128]
    pl.semaphore_wait(barrier, 2 * (GROUP - 1))
    mine = own.at[pl.ds(0, 3)]
    loop(1, 8, lambda d: image_row(own, d, row, same_core(d)).start())
    loop(1, 4, lambda d: image_col(mine, d, col, along_z(d)).start())
    image_row(own, 0, row, sibling).start()
    loop(1, 4, lambda d: image_col(mine, 3 + d, col, along_x(d)).start())
    vraw[row] = own[...]
    uraw[col] = own[0:3]

    def forward_x(d):
        slot = along_z(d)
        image_col(mine, 0, slot, slot).wait_recv()
        loop(1, 4, lambda e: image_col(uraw.at[slot], 3 + 3 * d + e, slot, along_x(e)).start())

    loop(1, 4, forward_x)

    def forward_core(d):
        slot = same_core(d)
        image_row(own, 0, slot, slot).wait_recv()
        image_row(vraw.at[slot], 7 + d, slot, sibling).start()

    loop(1, 8, forward_core)

    def landed_x(e):
        loop(0, 4, lambda d: image_col(mine, 0, (along_x(e) // 4) * 4 + d, col).wait_recv())

    loop(1, 4, landed_x)

    def prepare_rows(i):
        us = pl.ds(i * 4, 4)
        x = repeat_lanes(uraw[us], m)
        ui[us] = x
        for l, d in enumerate(self_maps(x, m)):
            r = lax.rsqrt(d)
            um[us, l] = d * r * (1.0 / (9.0 * PI) if l < 2 else 1.0)
            um[us, 3 + l] = r

    loop(0, 4, prepare_rows)
    loop(0, 8, lambda d: image_row(own, 0, 2 * d + lax.rem(row + 1, 2), row).wait_recv())
    for h in range(2):
        vs = pl.ds(4 * h, 4)
        x = pack_lanes(
            [vraw[pl.ds(8 * (j % 2) + 4 * h, 4), 3 * (j // 2) : 3 * (j // 2) + 3] for j in range(4)], m
        )
        vi[vs] = x * (1.0 / 27.0)
        for l, d in enumerate(self_maps(x, m)):
            r = lax.rsqrt(d)
            vm[vs, l] = d * r
            vm[vs, 3 + l] = r

    def forward(u, carry):
        k = box(ui[u, 0] * vi[:, 0] + ui[u, 1] * vi[:, 1] + ui[u, 2] * vi[:, 2], m) + BIAS
        for l in range(3):
            y = k * um[u, 3 + l]
            s, phi = arc(y * vm[:, 3 + l])
            s = s * vm[:, l]
            z = (s + phi * y) * um[u, l]
            phis[l, u] = phi
            sines[l, u] = s
            if l < 2:
                k = box(z, m) + BIAS
        total = jnp.sum(jnp.sum(z, axis=1), axis=1)
        for v in range(8):
            partial[v, pl.ds(u, 1), :] = total[v : v + 1]
        return carry

    lax.fori_loop(0, GROUP, forward, 0, unroll=2)

    tile = jnp.zeros((8, 128), F32)
    for half in range(2):
        for j in range(4):
            for v in range(8):
                part = partial[v, 8 * half : 8 * half + 8, :]
                total = jnp.sum(jnp.where(m["group"] == j, part, 0.0), axis=1, keepdims=True)
                lane = 16 * (2 * (j // 2) + half) + 8 * (j % 2) + v
                tile = jnp.where(m["lane"] == lane, total, tile)
    packed[col] = tile * (1.0 / (PIX * PI))
    packed[col, 0:1, 64 : 64 + CLASSES] = labels_ref[...]
    loop(1, GROUP, lambda d: tile_col(d, col, col_peer(d)).start())

    def backward(u, carry):
        g = box(phis[2, u], m)
        sines[1, u] = g * sines[1, u]
        g = box(g * phis[1, u], m)
        sines[0, u] = g * sines[0, u]
        phis[0, u] = box(g * phis[0, u], m)
        return carry

    lax.fori_loop(0, 6, backward, 0, unroll=2)
    loop(1, GROUP, lambda d: tile_col(d, col_peer(d), col).wait_recv())
    slot_of = m["lane"] // 16
    for kind, block in ((0, send_a), (1, send_b)):
        for half in range(2):
            for h in range(2):
                acc = jnp.zeros((8, 128), F32)
                for c in range(8):
                    moved = packed[8 * h + c]
                    turn = (c - 2 * kind - half) % 8
                    if turn:
                        moved = pltpu.roll(moved, 16 * turn, 1)
                    acc = jnp.where(slot_of == c, moved, acc)
                block[h, 8 * half : 8 * half + 8, :] = acc
    for c in range(GROUP):
        send_b[2, c : c + 1, :] = jnp.where(
            m["lane"][0:1] < CLASSES, pltpu.roll(packed[c, 0:1, :], 64, 1), 0.0
        )
    loop(1, GROUP, lambda d: block_a(d, row, row_peer(d)).start())
    loop(1, GROUP, lambda d: block_b(d, row, row_peer(d)).start())
    abuf[:, pl.ds(row * GROUP, GROUP)] = send_a[...]
    bbuf[:, pl.ds(row * GROUP, GROUP)] = send_b[...]
    lax.fori_loop(6, GROUP, backward, 0, unroll=2)

    rows = lax.broadcasted_iota(jnp.int32, (256, 256), 0)
    cols = lax.broadcasted_iota(jnp.int32, (256, 256), 1)
    identity = (rows == cols).astype(F32)
    permute = (rows == lax.rem(cols, GROUP) * GROUP + cols // GROUP).astype(BF16)
    class_row = lax.broadcasted_iota(jnp.int32, (16, 256), 0)
    onehot = (classes_ref[...] == class_row).astype(BF16)
    wanted = jnp.dot(onehot, permute, preferred_element_type=F32) - jnp.where(
        class_row < CLASSES, 1.0 / CLASSES, 0.0
    )
    loop(1, GROUP, lambda d: block_a(d, row_peer(d), row).wait_recv())
    ordered = lambda ref, part: jnp.concatenate(
        [ref[part, pl.ds(i, GROUP, stride=GROUP), :] for i in range(GROUP)], axis=0
    )
    kss = jnp.concatenate([ordered(abuf, 0), ordered(abuf, 1)], axis=1)
    trace = jnp.sum(jnp.sum(kss * identity, axis=0, keepdims=True), axis=1, keepdims=True) * (
        1.0 / SUPPORT
    )
    scale = 1.0 / trace
    system = kss * scale + RIDGE * identity
    inverse = invert(system, identity)

    def solve(rhs_t):
        first = dot6(rhs_t, inverse)
        return (first + dot6(rhs_t - dot6(first, system), inverse)) * scale

    loop(1, GROUP, lambda d: block_b(d, row_peer(d), row).wait_recv())
    labels_t = jnp.transpose(ordered(bbuf, 2))[0:16]
    kst = jnp.concatenate([ordered(bbuf, 0), ordered(bbuf, 1)], axis=1)
    alpha_t = solve(labels_t)
    error_t = dot6(alpha_t, kst) - wanted
    loss = jnp.sum(jnp.sum(error_t * error_t, axis=0, keepdims=True), axis=1, keepdims=True)
    loss_out[...] = 0.5 * loss
    gamma_t = solve(dot_nt(error_t, kst))
    inner = jnp.sum(jnp.sum(gamma_t * alpha_t, axis=0, keepdims=True), axis=1, keepdims=True)

    pad = jnp.zeros((80, 256), F32)
    side1[...] = jnp.transpose(jnp.concatenate([alpha_t, gamma_t, error_t, pad], axis=0))
    side2[...] = jnp.transpose(jnp.concatenate([-gamma_t, -alpha_t, alpha_t, pad], axis=0))
    column = side1[pl.ds(col * GROUP, GROUP), :]
    lane16 = lax.broadcasted_iota(jnp.int32, (16, 128), 1)
    sub16 = lax.broadcasted_iota(jnp.int32, (16, 128), 0)
    left = jnp.concatenate(
        [jnp.where(lane16 < 32, column, 0.0), jnp.where(lane16 < 32, 0.0, column)], axis=0
    )
    right = jnp.concatenate(
        [side2[pl.ds(row, GROUP, stride=GROUP), :], jnp.zeros((112, 128), F32)], axis=0
    )
    weights = dot_nt(left, right)
    on_diagonal = ((sub16 == row) & (lane16 == col)).astype(F32)
    weights = jnp.concatenate(
        [weights[0:16] - (2.0 * RIDGE / SUPPORT) * inner * on_diagonal, weights[16:32]], axis=0
    )
    own_row = side1[pl.ds(col * GROUP + row, 1), :]
    label_out[...] = own_row[:, 16 : 16 + CLASSES]
    for u in range(GROUP):
        y = weights[0:8, u : u + 1] * jnp.ones((8, 128), F32)
        for j in (1, 2, 3):
            y = jnp.where(m["group"] == j, weights[8 * j : 8 * j + 8, u : u + 1], y)
        wbuf[u] = y

    step9 = 1.0 / (9.0 * PI)
    each = 1.0 / (2.0 * PI * PIX)
    scale_image = 27.0 * step9**3 / (3.0 * PIX)

    def contract(u):
        sums = None
        for v in range(8):
            w = jnp.broadcast_to(wbuf[u, v : v + 1, :], (8, 128))
            g = w * phis[0, u, v]
            terms = [w * sines[l, u, v] for l in range(3)] + [g * vi[v, c] for c in range(3)]
            sums = terms if sums is None else [a + b for a, b in zip(sums, terms)]
        h = [sums[l] * um[u, 3 + l] * (each * step9 ** (2 - l)) for l in range(3)]
        return h, jnp.stack(sums[3:], axis=0) * scale_image, ui[u]

    def batch(b, last):
        us = [col_peer(1 + 4 * b + i) for i in range(4)]
        parts = [contract(u) for u in us]
        h1, h2, h3 = (jnp.stack([p[0][l] for p in parts], axis=0) for l in range(3))
        back = h1 + box(h2 + box(h3, m) * (1.0 / 9.0), m) * (1.0 / 9.0)
        back = box(back, m) * (2.0 / 27.0)
        image = jnp.stack([p[1] for p in parts], axis=0)
        x = jnp.stack([p[2] for p in parts], axis=0)
        out = merge_lanes(image + back[:, None] * x, m)
        for i, u in enumerate(us):
            if last and i == 3:
                grecv[col] = out[i]
            else:
                gsend[u] = out[i]
                grad_col(1 + 4 * b + i, col, u).start()

    loop(0, 3, lambda b: batch(b, False))
    batch(3, True)

    def sent_row(d):
        block_a(d, row, row_peer(d)).wait_send()
        block_b(d, row, row_peer(d)).wait_send()
        image_col(mine, d, col, col_peer(d)).wait_send()
        tile_col(d, col, col_peer(d)).wait_send()
        grad_col(d, col, col_peer(d)).wait_send()

    loop(1, GROUP, sent_row)
    loop(0, GROUP - 1, lambda k: image_row(own, k, row, sibling).wait_send())
    loop(1, GROUP, lambda d: grad_col(d, col_peer(d), col).wait_recv())
    total = grecv[0]
    for i in range(1, GROUP):
        total = total + grecv[i]
    for c in range(3):
        for k in range(8):
            grad_out[c, 0:1, k * 128 : (k + 1) * 128] = total[c, k : k + 1, :]


def body(support_views, support_pick, target_views, target_pick, support_labels, target_labels):
    vmem = pl.BlockSpec(memory_space=pltpu.VMEM)
    smem = pl.BlockSpec(memory_space=pltpu.SMEM)
    buf = lambda *shape: pltpu.VMEM(shape, F32)
    grad, label_grad, loss = pl.pallas_call(
        step_kernel,
        name="kip_step",
        out_shape=(
            jax.ShapeDtypeStruct((3, 1, PIX), F32),
            jax.ShapeDtypeStruct((1, CLASSES), F32),
            jax.ShapeDtypeStruct((1, 1), F32),
        ),
        in_specs=[vmem, smem, vmem, smem, vmem, vmem],
        out_specs=(vmem, vmem, vmem),
        scratch_shapes=[
            buf(6, 8, 128),
            buf(GROUP, 6, 8, 128),
            buf(GROUP, 3, 8, 128),
            buf(GROUP, 3, 4, 8, 128),
            buf(GROUP, 6, 4, 8, 128),
            buf(8, 3, 4, 8, 128),
            buf(8, 6, 4, 8, 128),
            buf(3, GROUP, 8, 4, 8, 128),
            buf(3, GROUP, 8, 4, 8, 128),
            buf(8, GROUP, 128),
            buf(GROUP, 8, 128),
            buf(2, GROUP, 128),
            buf(3, GROUP, 128),
            buf(2, 256, 128),
            buf(3, 256, 128),
            buf(256, 128),
            buf(256, 128),
            buf(GROUP, 8, 128),
            buf(GROUP, 3, 8, 128),
            buf(GROUP, 3, 8, 128),
        ]
        + [pltpu.SemaphoreType.DMA((GROUP,))] * 12,
        compiler_params=pltpu.CompilerParams(
            collective_id=0, has_side_effects=True, vmem_limit_bytes=56 << 20
        ),
    )(
        jnp.transpose(support_views, (0, 2, 1, 3)),
        support_pick,
        jnp.transpose(target_views, (0, 2, 1, 3)),
        target_pick,
        support_labels,
        target_labels.reshape(1, SUPPORT),
    )
    return jnp.transpose(grad, (1, 0, 2)), label_grad, loss.reshape(())


def solution(mesh):
    both = ("row", "col")
    return jax.shard_map(
        body,
        mesh=mesh,
        in_specs=(
            P(both, None, None, None),
            P(both),
            P(both, None, None, None),
            P(both),
            P(both, None),
            P(),
        ),
        out_specs=(P(both, None, None), P(both, None), P()),
        check_vma=False,
    )
```

```python
import jax
import jax.numpy as jnp
import numpy as np
from jax import lax
from jax.experimental import pallas as pl
from jax.experimental.pallas import tpu as pltpu
from jax.sharding import PartitionSpec as P

PI = float(np.pi)
BIAS = 0.1
RIDGE = 0.1
GROUP = 16
PIX = 1024
SUPPORT = 256
CLASSES = 10
HIGHEST = lax.Precision.HIGHEST
F32 = jnp.float32
BF16 = jnp.bfloat16
ACOS = (
    1.570796251296997,
    -0.21459108591079712,
    0.08883588761091232,
    -0.04919743537902832,
    0.027762912213802338,
    -0.012003393843770027,
    0.0026117200031876564,
)


def inverse_schedule():
    low, high = RIDGE * 0.99, SUPPORT + 2 * RIDGE
    first = 2.0 / (low + high)
    error = (high - low) / (high + low)
    scales = []
    while error > 2e-4:
        scales.append(2.0 / (2.0 - error * error))
        error = error * error / (2.0 - error * error)
    return first, scales


FIRST_SCALE, SCALES = inverse_schedule()
BEFORE = 10
assert GROUP - BEFORE <= 2 * (len(SCALES) - 1)


def make_masks():
    lane = lax.broadcasted_iota(jnp.int32, (8, 128), 1)
    sub = lax.broadcasted_iota(jnp.int32, (8, 128), 0)
    col = lane & 31
    return dict(
        right=(col < 31).astype(F32),
        left=(col > 0).astype(F32),
        below=(sub < 7).astype(F32),
        above=(sub > 0).astype(F32),
        group=lane // 32,
        lane=lane,
    )


def box(x, m):
    h = (
        x
        + m["right"] * pltpu.roll(x, 127, x.ndim - 1)
        + m["left"] * pltpu.roll(x, 1, x.ndim - 1)
    )
    h0, h1, h2, h3 = (h[..., k, :, :] for k in range(4))
    above = pltpu.roll(h3, 1, h3.ndim - 2) * m["above"]
    below = pltpu.roll(h0, 7, h3.ndim - 2) * m["below"]
    a = h0 + h1
    b = h2 + h3
    return jnp.stack([above + a, a + h2, h1 + b, b + below], axis=-3)


def arc(c):
    t = jnp.abs(c)
    w = jnp.maximum(1.0 - t, 1e-30)
    v = 1.0 + t
    q = w * lax.rsqrt(w)
    s = q * (v * lax.rsqrt(v))
    p = jnp.full_like(t, ACOS[-1])
    for a in ACOS[-2::-1]:
        p = p * t + a
    theta = q * p
    return s, jnp.where(c < 0, theta, PI - theta)


def repeat_lanes(x, m):
    rolled = [x] + [pltpu.roll(x, 32 * i, x.ndim - 1) for i in (1, 2, 3)]
    out = []
    for k in range(4):
        y = rolled[0]
        for i in (1, 2, 3):
            y = jnp.where(m["group"] == ((k + i) % 4), rolled[i], y)
        out.append(y)
    return jnp.stack(out, axis=-3)


def pack_lanes(maps, m):
    rolled = [[x if i == 0 else pltpu.roll(x, 32 * i, x.ndim - 1) for i in range(4)] for x in maps]
    out = []
    for k in range(4):
        y = rolled[0][(0 - k) % 4]
        for j in (1, 2, 3):
            y = jnp.where(m["group"] == j, rolled[j][(j - k) % 4], y)
        out.append(y)
    return jnp.stack(out, axis=-3)


def merge_lanes(x, m):
    last = x.ndim - 1
    x = x + pltpu.roll(x, 64, last)
    x = x + pltpu.roll(x, 32, last)
    y = x[..., 0, :, :]
    for k in (1, 2, 3):
        y = jnp.where(m["group"] == k, x[..., k, :, :], y)
    return y


def self_maps(x, m):
    d = box((x[:, 0] * x[:, 0] + x[:, 1] * x[:, 1] + x[:, 2] * x[:, 2]) * (1.0 / 27.0), m) + BIAS
    maps = [d]
    for _ in range(2):
        d = box(d, m) * (1.0 / 9.0) + BIAS
        maps.append(d)
    return maps


def dot3(a, b):
    ah = a.astype(BF16)
    al = (a - ah.astype(F32)).astype(BF16)
    bh = b.astype(BF16)
    bl = (b - bh.astype(F32)).astype(BF16)
    d = lambda p, q: jnp.dot(p, q, preferred_element_type=F32)
    return d(ah, bh) + (d(ah, bl) + d(al, bh))


def dot6(a, b):
    return jnp.dot(a, b, precision=HIGHEST, preferred_element_type=F32)


def dot_nt(a, b):
    return lax.dot_general(
        a, b, (((1,), (1,)), ((), ())), precision=HIGHEST, preferred_element_type=F32
    )


def invert(a, identity, beside):
    x = (SCALES[0] * FIRST_SCALE) * (2.0 * identity - FIRST_SCALE * a)
    count = len(SCALES)
    for i in range(1, count):
        mul = dot6 if i == count - 1 else dot3
        product = mul(a, x)
        beside(2 * i - 2)
        x = SCALES[i] * mul(x, 2.0 * identity - product)
        beside(2 * i - 1)
    return x


def step_kernel(
    views_ref,
    pick_ref,
    target_views_ref,
    target_pick_ref,
    labels_ref,
    classes_ref,
    grad_out,
    label_out,
    loss_out,
    own,
    vraw,
    uraw,
    ui,
    um,
    vi,
    vm,
    phis,
    sines,
    partial,
    packed,
    packed_b,
    send_a,
    send_b,
    abuf,
    bbuf,
    side1,
    side2,
    wleft,
    wbuf,
    gsend,
    grecv,
    img_row_s,
    img_row_r,
    img_tgt_s,
    img_tgt_r,
    img_col_s,
    img_col_r,
    t1_s,
    t1_r,
    t1b_s,
    t1b_r,
    t2a_s,
    t2a_r,
    t2b_s,
    t2b_r,
    fin_s,
    fin_r,
):
    mesh_row = lax.axis_index("row")
    mesh_col = lax.axis_index("col")
    row = (mesh_col // 4) * 4 + mesh_row // 4
    col = lax.rem(mesh_col, 4) * 4 + lax.rem(mesh_row, 4)
    m = make_masks()

    def device(r, c):
        return (lax.rem(r, 4) * 4 + lax.rem(c, 4), (r // 4) * 4 + c // 4)

    def row_peer(d):
        return lax.rem(row + d, GROUP)

    def col_peer(d):
        return lax.rem(col + d, GROUP)

    def loop(low, high, body):
        def step(d, carry):
            body(d)
            return carry

        lax.fori_loop(low, high, step, 0)

    def far_first(start):
        def pair(k):
            start(8 + k)
            start(7 - k)

        loop(0, 7, pair)
        start(15)

    def remote(src, dst, ssem, rsem, device):
        return pltpu.make_async_remote_copy(
            src_ref=src,
            dst_ref=dst,
            send_sem=ssem,
            recv_sem=rsem,
            device_id=device,
            device_id_type=pl.DeviceIdType.MESH,
        )

    mine = own.at[pl.ds(0, 3)]
    mine_tgt = own.at[pl.ds(3, 3)]

    def image_row(d, slot, peer):
        return remote(
            mine, vraw.at[slot, pl.ds(0, 3)], img_row_s.at[d], img_row_r.at[slot], device(peer, col)
        )

    def image_tgt(d, slot, peer):
        return remote(
            mine_tgt, vraw.at[slot, pl.ds(3, 3)], img_tgt_s.at[d], img_tgt_r.at[slot], device(peer, col)
        )

    def image_col(d, slot, peer):
        return remote(mine, uraw.at[slot], img_col_s.at[d], img_col_r.at[slot], device(row, peer))

    def tile_col(d, slot, peer):
        return remote(packed.at[col], packed.at[slot], t1_s.at[d], t1_r.at[slot], device(row, peer))

    def tile_col_b(d, slot, peer):
        return remote(packed_b.at[col], packed_b.at[slot], t1b_s.at[d], t1b_r.at[slot], device(row, peer))

    def block_a(d, slot, peer):
        return remote(
            send_a, abuf.at[:, pl.ds(slot * GROUP, GROUP)], t2a_s.at[d], t2a_r.at[slot], device(peer, col)
        )

    def block_b(d, slot, peer):
        return remote(
            send_b, bbuf.at[:, pl.ds(slot * GROUP, GROUP)], t2b_s.at[d], t2b_r.at[slot], device(peer, col)
        )

    def grad_col(d, slot, peer):
        return remote(gsend.at[peer], grecv.at[slot], fin_s.at[d], fin_r.at[slot], device(row, peer))

    barrier = pltpu.get_barrier_semaphore()

    def greet(d):
        pl.semaphore_signal(
            barrier, inc=1, device_id=device(row, col_peer(d)), device_id_type=pl.DeviceIdType.MESH
        )
        pl.semaphore_signal(
            barrier, inc=1, device_id=device(row_peer(d), col), device_id_type=pl.DeviceIdType.MESH
        )

    loop(1, GROUP, greet)

    for c in range(3):
        support = views_ref[0, c, pl.ds(pick_ref[0], 1), :]
        target = target_views_ref[0, c, pl.ds(target_pick_ref[0], 1), :]
        for k in range(8):
            own[c, k : k + 1, :] = support[:, k * 128 : (k + 1) * 128]
            own[3 + c, k : k + 1, :] = target[:, k * 128 : (k + 1) * 128]
    pl.semaphore_wait(barrier, 2 * (GROUP - 1))
    far_first(lambda d: image_col(d, col, col_peer(d)).start())
    far_first(lambda d: image_row(d, row, row_peer(d)).start())
    far_first(lambda d: image_tgt(d, row, row_peer(d)).start())
    vraw[row] = own[...]
    uraw[col] = own[0:3]
    loop(1, GROUP, lambda d: image_col(d, col_peer(d), col).wait_recv())

    def prepare_rows(i):
        us = pl.ds(i * 4, 4)
        x = repeat_lanes(uraw[us], m)
        ui[us] = x
        for l, d in enumerate(self_maps(x, m)):
            r = lax.rsqrt(d)
            um[us, l] = d * r * (1.0 / (9.0 * PI) if l < 2 else 1.0)
            um[us, 3 + l] = r

    loop(0, 4, prepare_rows)

    def prepare_columns(kind):
        vs = slice(4 * kind, 4 * kind + 4)
        x = pack_lanes([vraw[4 * j : 4 * j + 4, 3 * kind : 3 * kind + 3] for j in range(4)], m)
        vi[vs] = x * (1.0 / 27.0)
        for l, d in enumerate(self_maps(x, m)):
            r = lax.rsqrt(d)
            vm[vs, l] = d * r
            vm[vs, 3 + l] = r

    loop(1, GROUP, lambda d: image_row(d, row_peer(d), row).wait_recv())
    prepare_columns(0)

    def forward(kind):
        vs = slice(4 * kind, 4 * kind + 4)

        def one(u, carry):
            k = box(ui[u, 0] * vi[vs, 0] + ui[u, 1] * vi[vs, 1] + ui[u, 2] * vi[vs, 2], m) + BIAS
            for l in range(3):
                y = k * um[u, 3 + l]
                s, phi = arc(y * vm[vs, 3 + l])
                s = s * vm[vs, l]
                z = (s + phi * y) * um[u, l]
                phis[l, u, vs] = phi
                sines[l, u, vs] = s
                if l < 2:
                    k = box(z, m) + BIAS
            total = jnp.sum(jnp.sum(z, axis=1), axis=1)
            for v in range(4):
                partial[4 * kind + v, pl.ds(u, 1), :] = total[v : v + 1]
            return carry

        lax.fori_loop(0, GROUP, one, 0, unroll=4)

    def pack_tile(kind):
        tile = jnp.zeros((8, 128), F32)
        for half in range(2):
            for j in range(4):
                for v in range(4):
                    part = partial[4 * kind + v, 8 * half : 8 * half + 8, :]
                    total = jnp.sum(jnp.where(m["group"] == j, part, 0.0), axis=1, keepdims=True)
                    tile = jnp.where(m["lane"] == 16 * half + 4 * j + v, total, tile)
        return tile * (1.0 / (PIX * PI))

    def assemble(tiles, block):
        for half in range(2):
            for h in range(2):
                acc = jnp.zeros((8, 128), F32)
                for c in range(8):
                    moved = tiles[8 * h + c]
                    turn = (c - half) % 8
                    if turn:
                        moved = pltpu.roll(moved, 16 * turn, 1)
                    acc = jnp.where(m["lane"] // 16 == c, moved, acc)
                block[h, 8 * half : 8 * half + 8, :] = acc

    def backward(u, carry):
        g = box(phis[2, u], m)
        sines[1, u] = g * sines[1, u]
        g = box(g * phis[1, u], m)
        sines[0, u] = g * sines[0, u]
        phis[0, u] = box(g * phis[0, u], m)
        return carry

    forward(0)
    packed[col] = pack_tile(0)
    packed[col, 0:1, 64 : 64 + CLASSES] = labels_ref[...]
    far_first(lambda d: tile_col(d, col, col_peer(d)).start())
    loop(1, GROUP, lambda d: image_tgt(d, row_peer(d), row).wait_recv())
    prepare_columns(1)
    forward(1)
    packed_b[col] = pack_tile(1)
    far_first(lambda d: tile_col_b(d, col, col_peer(d)).start())
    loop(1, GROUP, lambda d: tile_col(d, col_peer(d), col).wait_recv())
    assemble(packed, send_a)
    far_first(lambda d: block_a(d, row, row_peer(d)).start())
    abuf[:, pl.ds(row * GROUP, GROUP)] = send_a[...]
    for c in range(GROUP):
        send_b[2, c : c + 1, :] = jnp.where(
            m["lane"][0:1] < CLASSES, pltpu.roll(packed[c, 0:1, :], 64, 1), 0.0
        )
    lax.fori_loop(0, BEFORE, backward, 0, unroll=2)
    loop(1, GROUP, lambda d: tile_col_b(d, col_peer(d), col).wait_recv())
    assemble(packed_b, send_b)
    far_first(lambda d: block_b(d, row, row_peer(d)).start())
    bbuf[:, pl.ds(row * GROUP, GROUP)] = send_b[...]

    rows = lax.broadcasted_iota(jnp.int32, (256, 256), 0)
    cols = lax.broadcasted_iota(jnp.int32, (256, 256), 1)
    identity = (rows == cols).astype(F32)
    there_col = lax.rem(rows, GROUP)
    there_row = rows // GROUP
    place = (lax.rem(there_col, 4) * 4 + lax.rem(there_row, 4)) * GROUP + (
        (there_col // 4) * 4 + there_row // 4
    )
    permute = (cols == place).astype(BF16)
    class_row = lax.broadcasted_iota(jnp.int32, (16, 256), 0)
    onehot = (classes_ref[...] == class_row).astype(BF16)
    wanted = jnp.dot(onehot, permute, preferred_element_type=F32) - jnp.where(
        class_row < CLASSES, 1.0 / CLASSES, 0.0
    )
    loop(1, GROUP, lambda d: block_a(d, row_peer(d), row).wait_recv())
    ordered = lambda ref, part: jnp.concatenate(
        [ref[part, pl.ds(i, GROUP, stride=GROUP), :] for i in range(GROUP)], axis=0
    )
    kss = jnp.concatenate([ordered(abuf, 0), ordered(abuf, 1)], axis=1)
    trace = jnp.sum(jnp.sum(kss * identity, axis=0, keepdims=True), axis=1, keepdims=True) * (
        1.0 / SUPPORT
    )
    scale = 1.0 / trace
    system = kss * scale + RIDGE * identity

    def beside(i):
        if BEFORE + i < GROUP:
            backward(BEFORE + i, 0)

    inverse = invert(system, identity, beside)

    def solve(rhs_t):
        first = dot6(rhs_t, inverse)
        return (first + dot6(rhs_t - dot6(first, system), inverse)) * scale

    loop(1, GROUP, lambda d: block_b(d, row_peer(d), row).wait_recv())
    labels_t = jnp.transpose(ordered(bbuf, 2))[0:16]
    kst = jnp.concatenate([ordered(bbuf, 0), ordered(bbuf, 1)], axis=1)
    alpha_t = solve(labels_t)
    error_t = dot6(alpha_t, kst) - wanted
    loss = jnp.sum(jnp.sum(error_t * error_t, axis=0, keepdims=True), axis=1, keepdims=True)
    loss_out[...] = 0.5 * loss
    gamma_t = solve(dot_nt(error_t, kst))
    inner = jnp.sum(jnp.sum(gamma_t * alpha_t, axis=0, keepdims=True), axis=1, keepdims=True)

    pad = jnp.zeros((80, 256), F32)
    side1[...] = jnp.transpose(jnp.concatenate([alpha_t, gamma_t, error_t, pad], axis=0))
    side2[...] = jnp.transpose(jnp.concatenate([-gamma_t, -alpha_t, alpha_t, pad], axis=0))
    column = side1[pl.ds(col * GROUP, GROUP), :]
    lane16 = lax.broadcasted_iota(jnp.int32, (16, 128), 1)
    for kind in range(2):
        masked = jnp.where((lane16 < 32) == (kind == 0), column, 0.0)
        for j in range(4):
            wleft[8 * j + 4 * kind : 8 * j + 4 * kind + 4, :] = masked[4 * j : 4 * j + 4]
    right = jnp.concatenate(
        [side2[pl.ds(row, GROUP, stride=GROUP), :], jnp.zeros((112, 128), F32)], axis=0
    )
    weights = dot_nt(wleft[...], right)
    lane32 = lax.broadcasted_iota(jnp.int32, (32, 128), 1)
    sub32 = lax.broadcasted_iota(jnp.int32, (32, 128), 0)
    on_diagonal = ((sub32 == 8 * (row // 4) + lax.rem(row, 4)) & (lane32 == col)).astype(F32)
    weights = weights - (2.0 * RIDGE / SUPPORT) * inner * on_diagonal
    own_row = side1[pl.ds(col * GROUP + row, 1), :]
    label_out[...] = own_row[:, 16 : 16 + CLASSES]
    for u in range(GROUP):
        y = weights[0:8, u : u + 1] * jnp.ones((8, 128), F32)
        for j in (1, 2, 3):
            y = jnp.where(m["group"] == j, weights[8 * j : 8 * j + 8, u : u + 1], y)
        wbuf[u] = y

    step9 = 1.0 / (9.0 * PI)
    each = 1.0 / (2.0 * PI * PIX)
    scale_image = 27.0 * step9**3 / (3.0 * PIX)

    def contract(u):
        sums = None
        for v in range(8):
            w = jnp.broadcast_to(wbuf[u, v : v + 1, :], (8, 128))
            g = w * phis[0, u, v]
            terms = [w * sines[l, u, v] for l in range(3)] + [g * vi[v, c] for c in range(3)]
            sums = terms if sums is None else [a + b for a, b in zip(sums, terms)]
        h = [sums[l] * um[u, 3 + l] * (each * step9 ** (2 - l)) for l in range(3)]
        return h, jnp.stack(sums[3:], axis=0) * scale_image, ui[u]

    def batch(b, last):
        places = [8 + 2 * b + i // 2 if i % 2 == 0 else 8 - 2 * b - (i + 1) // 2 for i in range(4)]
        us = [col_peer(d) for d in places]
        parts = [contract(u) for u in us]
        h1, h2, h3 = (jnp.stack([p[0][l] for p in parts], axis=0) for l in range(3))
        back = h1 + box(h2 + box(h3, m) * (1.0 / 9.0), m) * (1.0 / 9.0)
        back = box(back, m) * (2.0 / 27.0)
        image = jnp.stack([p[1] for p in parts], axis=0)
        x = jnp.stack([p[2] for p in parts], axis=0)
        out = merge_lanes(image + back[:, None] * x, m)
        for i, u in enumerate(us):
            if last and i == 3:
                grecv[col] = out[i]
            else:
                gsend[u] = out[i]
                grad_col(places[i], col, u).start()

    loop(0, 3, lambda b: batch(b, False))
    batch(3, True)

    def sent_row(d):
        block_a(d, row, row_peer(d)).wait_send()
        block_b(d, row, row_peer(d)).wait_send()
        image_col(d, col, col_peer(d)).wait_send()
        image_row(d, row, row_peer(d)).wait_send()
        image_tgt(d, row, row_peer(d)).wait_send()
        tile_col(d, col, col_peer(d)).wait_send()
        tile_col_b(d, col, col_peer(d)).wait_send()
        grad_col(d, col, col_peer(d)).wait_send()

    loop(1, GROUP, sent_row)
    loop(1, GROUP, lambda d: grad_col(d, col_peer(d), col).wait_recv())
    total = grecv[0]
    for i in range(1, GROUP):
        total = total + grecv[i]
    for c in range(3):
        for k in range(8):
            grad_out[c, 0:1, k * 128 : (k + 1) * 128] = total[c, k : k + 1, :]


def body(support_views, support_pick, target_views, target_pick, support_labels, target_labels):
    vmem = pl.BlockSpec(memory_space=pltpu.VMEM)
    smem = pl.BlockSpec(memory_space=pltpu.SMEM)
    buf = lambda *shape: pltpu.VMEM(shape, F32)
    grad, label_grad, loss = pl.pallas_call(
        step_kernel,
        name="kip_step",
        out_shape=(
            jax.ShapeDtypeStruct((3, 1, PIX), F32),
            jax.ShapeDtypeStruct((1, CLASSES), F32),
            jax.ShapeDtypeStruct((1, 1), F32),
        ),
        in_specs=[vmem, smem, vmem, smem, vmem, vmem],
        out_specs=(vmem, vmem, vmem),
        scratch_shapes=[
            buf(6, 8, 128),
            buf(GROUP, 6, 8, 128),
            buf(GROUP, 3, 8, 128),
            buf(GROUP, 3, 4, 8, 128),
            buf(GROUP, 6, 4, 8, 128),
            buf(8, 3, 4, 8, 128),
            buf(8, 6, 4, 8, 128),
            buf(3, GROUP, 8, 4, 8, 128),
            buf(3, GROUP, 8, 4, 8, 128),
            buf(8, GROUP, 128),
            buf(GROUP, 8, 128),
            buf(GROUP, 8, 128),
            buf(2, GROUP, 128),
            buf(3, GROUP, 128),
            buf(2, 256, 128),
            buf(3, 256, 128),
            buf(256, 128),
            buf(256, 128),
            buf(32, 128),
            buf(GROUP, 8, 128),
            buf(GROUP, 3, 8, 128),
            buf(GROUP, 3, 8, 128),
        ]
        + [pltpu.SemaphoreType.DMA((GROUP,))] * 16,
        compiler_params=pltpu.CompilerParams(
            collective_id=0, has_side_effects=True, vmem_limit_bytes=56 << 20
        ),
    )(
        jnp.transpose(support_views, (0, 2, 1, 3)),
        support_pick,
        jnp.transpose(target_views, (0, 2, 1, 3)),
        target_pick,
        support_labels,
        target_labels.reshape(1, SUPPORT),
    )
    return jnp.transpose(grad, (1, 0, 2)), label_grad, loss.reshape(())


def solution(mesh):
    both = ("row", "col")
    return jax.shard_map(
        body,
        mesh=mesh,
        in_specs=(
            P(both, None, None, None),
            P(both),
            P(both, None, None, None),
            P(both),
            P(both, None),
            P(),
        ),
        out_specs=(P(both, None, None), P(both, None), P()),
        check_vma=False,
    )
```

```python
import jax
import jax.numpy as jnp
import numpy as np
from jax import lax
from jax.experimental import pallas as pl
from jax.experimental.pallas import tpu as pltpu
from jax.sharding import PartitionSpec as P

PI = float(np.pi)
BIAS = 0.1
RIDGE = 0.1
GROUP = 16
PIX = 1024
SUPPORT = 256
CLASSES = 10
HIGHEST = lax.Precision.HIGHEST
F32 = jnp.float32
BF16 = jnp.bfloat16
ACOS = (
    1.570796251296997,
    -0.21459108591079712,
    0.08883588761091232,
    -0.04919743537902832,
    0.027762912213802338,
    -0.012003393843770027,
    0.0026117200031876564,
)


def inverse_schedule():
    low, high = RIDGE * 0.99, SUPPORT + 2 * RIDGE
    first = 2.0 / (low + high)
    error = (high - low) / (high + low)
    scales = []
    while error > 2e-4:
        scales.append(2.0 / (2.0 - error * error))
        error = error * error / (2.0 - error * error)
    return first, scales


FIRST_SCALE, SCALES = inverse_schedule()
BEFORE = 10
SPLIT = 8
assert GROUP - BEFORE <= 2 * (len(SCALES) - 1)


def make_masks():
    lane = lax.broadcasted_iota(jnp.int32, (8, 128), 1)
    sub = lax.broadcasted_iota(jnp.int32, (8, 128), 0)
    col = lane & 31
    return dict(
        right=(col < 31).astype(F32),
        left=(col > 0).astype(F32),
        below=(sub < 7).astype(F32),
        above=(sub > 0).astype(F32),
        group=lane // 32,
        lane=lane,
    )


def box(x, m):
    h = (
        x
        + m["right"] * pltpu.roll(x, 127, x.ndim - 1)
        + m["left"] * pltpu.roll(x, 1, x.ndim - 1)
    )
    h0, h1, h2, h3 = (h[..., k, :, :] for k in range(4))
    above = pltpu.roll(h3, 1, h3.ndim - 2) * m["above"]
    below = pltpu.roll(h0, 7, h3.ndim - 2) * m["below"]
    a = h0 + h1
    b = h2 + h3
    return jnp.stack([above + a, a + h2, h1 + b, b + below], axis=-3)


def arc(c):
    t = jnp.abs(c)
    w = jnp.maximum(1.0 - t, 1e-30)
    v = 1.0 + t
    q = w * lax.rsqrt(w)
    s = q * (v * lax.rsqrt(v))
    p = jnp.full_like(t, ACOS[-1])
    for a in ACOS[-2::-1]:
        p = p * t + a
    theta = q * p
    return s, jnp.where(c < 0, theta, PI - theta)


def repeat_lanes(x, m):
    rolled = [x] + [pltpu.roll(x, 32 * i, x.ndim - 1) for i in (1, 2, 3)]
    out = []
    for k in range(4):
        y = rolled[0]
        for i in (1, 2, 3):
            y = jnp.where(m["group"] == ((k + i) % 4), rolled[i], y)
        out.append(y)
    return jnp.stack(out, axis=-3)


def pack_lanes(maps, m):
    rolled = [[x if i == 0 else pltpu.roll(x, 32 * i, x.ndim - 1) for i in range(4)] for x in maps]
    out = []
    for k in range(4):
        y = rolled[0][(0 - k) % 4]
        for j in (1, 2, 3):
            y = jnp.where(m["group"] == j, rolled[j][(j - k) % 4], y)
        out.append(y)
    return jnp.stack(out, axis=-3)


def merge_lanes(x, m):
    last = x.ndim - 1
    x = x + pltpu.roll(x, 64, last)
    x = x + pltpu.roll(x, 32, last)
    y = x[..., 0, :, :]
    for k in (1, 2, 3):
        y = jnp.where(m["group"] == k, x[..., k, :, :], y)
    return y


def self_maps(x, m):
    d = box((x[:, 0] * x[:, 0] + x[:, 1] * x[:, 1] + x[:, 2] * x[:, 2]) * (1.0 / 27.0), m) + BIAS
    maps = [d]
    for _ in range(2):
        d = box(d, m) * (1.0 / 9.0) + BIAS
        maps.append(d)
    return maps


def dot3(a, b):
    ah = a.astype(BF16)
    al = (a - ah.astype(F32)).astype(BF16)
    bh = b.astype(BF16)
    bl = (b - bh.astype(F32)).astype(BF16)
    d = lambda p, q: jnp.dot(p, q, preferred_element_type=F32)
    return d(ah, bh) + (d(ah, bl) + d(al, bh))


def dot6(a, b):
    return jnp.dot(a, b, precision=HIGHEST, preferred_element_type=F32)


def dot_nt(a, b):
    return lax.dot_general(
        a, b, (((1,), (1,)), ((), ())), precision=HIGHEST, preferred_element_type=F32
    )


def invert(a, identity, beside):
    x = (SCALES[0] * FIRST_SCALE) * (2.0 * identity - FIRST_SCALE * a)
    count = len(SCALES)
    for i in range(1, count):
        mul = dot6 if i >= count - 1 else dot3
        product = mul(a, x)
        beside(2 * i - 2)
        x = SCALES[i] * mul(x, 2.0 * identity - product)
        beside(2 * i - 1)
    return x


def step_kernel(
    views_ref,
    pick_ref,
    target_views_ref,
    target_pick_ref,
    labels_ref,
    classes_ref,
    grad_out,
    label_out,
    loss_out,
    own,
    vraw,
    uraw,
    ui,
    um,
    vi,
    vm,
    phis,
    sines,
    partial,
    packed,
    packed_b,
    send_a,
    send_b,
    abuf,
    bbuf,
    side1,
    side2,
    wleft,
    wbuf,
    gsend,
    grecv,
    img_row_s,
    img_row_r,
    img_tgt_s,
    img_tgt_r,
    img_col_s,
    img_col_r,
    t1_s,
    t1_r,
    t1b_s,
    t1b_r,
    t2a_s,
    t2a_r,
    t2b_s,
    t2b_r,
    fin_s,
    fin_r,
):
    mesh_row = lax.axis_index("row")
    mesh_col = lax.axis_index("col")
    row = (mesh_col // 4) * 4 + mesh_row // 4
    col = lax.rem(mesh_col, 4) * 4 + lax.rem(mesh_row, 4)
    m = make_masks()

    def device(r, c):
        return (lax.rem(r, 4) * 4 + lax.rem(c, 4), (r // 4) * 4 + c // 4)

    def row_peer(d):
        return lax.rem(row + d, GROUP)

    def col_peer(d):
        return lax.rem(col + d, GROUP)

    def loop(low, high, body):
        def step(d, carry):
            body(d)
            return carry

        lax.fori_loop(low, high, step, 0)

    def far_first(start):
        def pair(k):
            start(8 + k)
            start(7 - k)

        loop(0, 7, pair)
        start(15)

    def remote(src, dst, ssem, rsem, device):
        return pltpu.make_async_remote_copy(
            src_ref=src,
            dst_ref=dst,
            send_sem=ssem,
            recv_sem=rsem,
            device_id=device,
            device_id_type=pl.DeviceIdType.MESH,
        )

    mine = own.at[pl.ds(0, 3)]
    mine_tgt = own.at[pl.ds(3, 3)]

    def image_row(d, slot, peer):
        return remote(
            mine, vraw.at[slot, pl.ds(0, 3)], img_row_s.at[d], img_row_r.at[slot], device(peer, col)
        )

    def image_tgt(d, slot, peer):
        return remote(
            mine_tgt, vraw.at[slot, pl.ds(3, 3)], img_tgt_s.at[d], img_tgt_r.at[slot], device(peer, col)
        )

    def image_col(d, slot, peer):
        return remote(mine, uraw.at[slot], img_col_s.at[d], img_col_r.at[slot], device(row, peer))

    def tile_col(d, slot, peer):
        return remote(packed.at[col], packed.at[slot], t1_s.at[d], t1_r.at[slot], device(row, peer))

    def tile_col_b(d, slot, peer):
        return remote(packed_b.at[col], packed_b.at[slot], t1b_s.at[d], t1b_r.at[slot], device(row, peer))

    def block_a(d, slot, peer):
        return remote(
            send_a, abuf.at[:, pl.ds(slot * GROUP, GROUP)], t2a_s.at[d], t2a_r.at[slot], device(peer, col)
        )

    def block_b(d, slot, peer):
        return remote(
            send_b, bbuf.at[:, pl.ds(slot * GROUP, GROUP)], t2b_s.at[d], t2b_r.at[slot], device(peer, col)
        )

    def grad_col(d, slot, peer):
        return remote(gsend.at[peer], grecv.at[slot], fin_s.at[d], fin_r.at[slot], device(row, peer))

    barrier = pltpu.get_barrier_semaphore()

    def greet(d):
        pl.semaphore_signal(
            barrier, inc=1, device_id=device(row, col_peer(d)), device_id_type=pl.DeviceIdType.MESH
        )
        pl.semaphore_signal(
            barrier, inc=1, device_id=device(row_peer(d), col), device_id_type=pl.DeviceIdType.MESH
        )

    loop(1, GROUP, greet)

    for c in range(3):
        support = views_ref[0, c, pl.ds(pick_ref[0], 1), :]
        target = target_views_ref[0, c, pl.ds(target_pick_ref[0], 1), :]
        for k in range(8):
            own[c, k : k + 1, :] = support[:, k * 128 : (k + 1) * 128]
            own[3 + c, k : k + 1, :] = target[:, k * 128 : (k + 1) * 128]
    pl.semaphore_wait(barrier, 2 * (GROUP - 1))
    far_first(lambda d: image_col(d, col, col_peer(d)).start())
    far_first(lambda d: image_row(d, row, row_peer(d)).start())
    far_first(lambda d: image_tgt(d, row, row_peer(d)).start())
    vraw[row] = own[...]
    uraw[col] = own[0:3]
    loop(1, GROUP, lambda d: image_col(d, col_peer(d), col).wait_recv())

    def prepare_rows(i):
        us = pl.ds(i * 4, 4)
        x = repeat_lanes(uraw[us], m)
        ui[us] = x
        for l, d in enumerate(self_maps(x, m)):
            r = lax.rsqrt(d)
            um[us, l] = d * r * (1.0 / (9.0 * PI) if l < 2 else 1.0)
            um[us, 3 + l] = r

    loop(0, 4, prepare_rows)

    def prepare_columns(kind):
        vs = slice(4 * kind, 4 * kind + 4)
        x = pack_lanes([vraw[4 * j : 4 * j + 4, 3 * kind : 3 * kind + 3] for j in range(4)], m)
        vi[vs] = x * (1.0 / 27.0)
        for l, d in enumerate(self_maps(x, m)):
            r = lax.rsqrt(d)
            vm[vs, l] = d * r
            vm[vs, 3 + l] = r

    loop(1, GROUP, lambda d: image_row(d, row_peer(d), row).wait_recv())
    prepare_columns(0)

    def forward(kind, low, high):
        vs = slice(4 * kind, 4 * kind + 4)

        def one(u, carry):
            k = box(ui[u, 0] * vi[vs, 0] + ui[u, 1] * vi[vs, 1] + ui[u, 2] * vi[vs, 2], m) + BIAS
            for l in range(3):
                y = k * um[u, 3 + l]
                s, phi = arc(y * vm[vs, 3 + l])
                s = s * vm[vs, l]
                z = (s + phi * y) * um[u, l]
                phis[l, u, vs] = phi
                sines[l, u, vs] = s
                if l < 2:
                    k = box(z, m) + BIAS
            total = jnp.sum(jnp.sum(z, axis=1), axis=1)
            for v in range(4):
                partial[4 * kind + v, pl.ds(u, 1), :] = total[v : v + 1]
            return carry

        lax.fori_loop(low, high, one, 0, unroll=4)

    def pack_tile(kind):
        tile = jnp.zeros((8, 128), F32)
        for half in range(2):
            for j in range(4):
                for v in range(4):
                    part = partial[4 * kind + v, 8 * half : 8 * half + 8, :]
                    total = jnp.sum(jnp.where(m["group"] == j, part, 0.0), axis=1, keepdims=True)
                    tile = jnp.where(m["lane"] == 16 * half + 4 * j + v, total, tile)
        return tile * (1.0 / (PIX * PI))

    def assemble(tiles, block):
        for half in range(2):
            for h in range(2):
                acc = jnp.zeros((8, 128), F32)
                for c in range(8):
                    moved = tiles[8 * h + c]
                    turn = (c - half) % 8
                    if turn:
                        moved = pltpu.roll(moved, 16 * turn, 1)
                    acc = jnp.where(m["lane"] // 16 == c, moved, acc)
                block[h, 8 * half : 8 * half + 8, :] = acc

    def backward(u, carry):
        g = box(phis[2, u], m)
        sines[1, u] = g * sines[1, u]
        g = box(g * phis[1, u], m)
        sines[0, u] = g * sines[0, u]
        phis[0, u] = box(g * phis[0, u], m)
        return carry

    forward(0, 0, GROUP)
    packed[col] = pack_tile(0)
    packed[col, 0:1, 64 : 64 + CLASSES] = labels_ref[...]
    far_first(lambda d: tile_col(d, col, col_peer(d)).start())
    loop(1, GROUP, lambda d: image_tgt(d, row_peer(d), row).wait_recv())
    prepare_columns(1)
    forward(1, 0, SPLIT)
    loop(1, GROUP, lambda d: tile_col(d, col_peer(d), col).wait_recv())
    assemble(packed, send_a)
    for c in range(GROUP):
        send_a[2, c : c + 1, :] = jnp.where(
            m["lane"][0:1] < CLASSES, pltpu.roll(packed[c, 0:1, :], 64, 1), 0.0
        )
    far_first(lambda d: block_a(d, row, row_peer(d)).start())
    abuf[:, pl.ds(row * GROUP, GROUP)] = send_a[...]
    forward(1, SPLIT, GROUP)
    packed_b[col] = pack_tile(1)
    far_first(lambda d: tile_col_b(d, col, col_peer(d)).start())
    lax.fori_loop(0, BEFORE, backward, 0, unroll=2)
    loop(1, GROUP, lambda d: tile_col_b(d, col_peer(d), col).wait_recv())
    assemble(packed_b, send_b)
    far_first(lambda d: block_b(d, row, row_peer(d)).start())
    bbuf[:, pl.ds(row * GROUP, GROUP)] = send_b[...]

    rows = lax.broadcasted_iota(jnp.int32, (256, 256), 0)
    cols = lax.broadcasted_iota(jnp.int32, (256, 256), 1)
    identity = (rows == cols).astype(F32)
    there_col = lax.rem(rows, GROUP)
    there_row = rows // GROUP
    place = (lax.rem(there_col, 4) * 4 + lax.rem(there_row, 4)) * GROUP + (
        (there_col // 4) * 4 + there_row // 4
    )
    permute = (cols == place).astype(BF16)
    class_row = lax.broadcasted_iota(jnp.int32, (16, 256), 0)
    onehot = (classes_ref[...] == class_row).astype(BF16)
    wanted = jnp.dot(onehot, permute, preferred_element_type=F32) - jnp.where(
        class_row < CLASSES, 1.0 / CLASSES, 0.0
    )
    loop(1, GROUP, lambda d: block_a(d, row_peer(d), row).wait_recv())
    ordered = lambda ref, part: jnp.concatenate(
        [ref[part, pl.ds(i, GROUP, stride=GROUP), :] for i in range(GROUP)], axis=0
    )
    kss = jnp.concatenate([ordered(abuf, 0), ordered(abuf, 1)], axis=1)
    trace = jnp.sum(jnp.sum(kss * identity, axis=0, keepdims=True), axis=1, keepdims=True) * (
        1.0 / SUPPORT
    )
    scale = 1.0 / trace
    system = kss * scale + RIDGE * identity

    def beside(i):
        if BEFORE + i < GROUP:
            backward(BEFORE + i, 0)

    inverse = invert(system, identity, beside)

    labels_t = jnp.transpose(ordered(abuf, 2))[0:16]
    alpha_t = dot6(labels_t, inverse)
    alpha_t = (alpha_t + dot6(labels_t - dot6(alpha_t, system), inverse)) * scale
    loop(1, GROUP, lambda d: block_b(d, row_peer(d), row).wait_recv())
    kst = jnp.concatenate([ordered(bbuf, 0), ordered(bbuf, 1)], axis=1)
    error_t = dot6(alpha_t, kst) - wanted
    loss = jnp.sum(jnp.sum(error_t * error_t, axis=0, keepdims=True), axis=1, keepdims=True)
    loss_out[...] = 0.5 * loss
    rhs_t = dot_nt(error_t, kst)
    gamma_t = dot6(rhs_t, inverse)
    gamma_t = (gamma_t + dot6(rhs_t - dot6(gamma_t, system), inverse)) * scale
    inner = jnp.sum(jnp.sum(gamma_t * alpha_t, axis=0, keepdims=True), axis=1, keepdims=True)

    pad = jnp.zeros((80, 256), F32)
    side1[...] = jnp.transpose(jnp.concatenate([alpha_t, gamma_t, error_t, pad], axis=0))
    side2[...] = jnp.transpose(jnp.concatenate([-gamma_t, -alpha_t, alpha_t, pad], axis=0))
    column = side1[pl.ds(col * GROUP, GROUP), :]
    lane16 = lax.broadcasted_iota(jnp.int32, (16, 128), 1)
    for kind in range(2):
        masked = jnp.where((lane16 < 32) == (kind == 0), column, 0.0)
        for j in range(4):
            wleft[8 * j + 4 * kind : 8 * j + 4 * kind + 4, :] = masked[4 * j : 4 * j + 4]
    right = jnp.concatenate(
        [side2[pl.ds(row, GROUP, stride=GROUP), :], jnp.zeros((112, 128), F32)], axis=0
    )
    weights = dot_nt(wleft[...], right)
    lane32 = lax.broadcasted_iota(jnp.int32, (32, 128), 1)
    sub32 = lax.broadcasted_iota(jnp.int32, (32, 128), 0)
    on_diagonal = ((sub32 == 8 * (row // 4) + lax.rem(row, 4)) & (lane32 == col)).astype(F32)
    weights = weights - (2.0 * RIDGE / SUPPORT) * inner * on_diagonal
    own_row = side1[pl.ds(col * GROUP + row, 1), :]
    label_out[...] = own_row[:, 16 : 16 + CLASSES]
    for u in range(GROUP):
        y = weights[0:8, u : u + 1] * jnp.ones((8, 128), F32)
        for j in (1, 2, 3):
            y = jnp.where(m["group"] == j, weights[8 * j : 8 * j + 8, u : u + 1], y)
        wbuf[u] = y

    step9 = 1.0 / (9.0 * PI)
    each = 1.0 / (2.0 * PI * PIX)
    scale_image = 27.0 * step9**3 / (3.0 * PIX)

    def contract(u):
        sums = None
        for v in range(8):
            w = jnp.broadcast_to(wbuf[u, v : v + 1, :], (8, 128))
            g = w * phis[0, u, v]
            terms = [w * sines[l, u, v] for l in range(3)] + [g * vi[v, c] for c in range(3)]
            sums = terms if sums is None else [a + b for a, b in zip(sums, terms)]
        h = [sums[l] * um[u, 3 + l] * (each * step9 ** (2 - l)) for l in range(3)]
        return h, jnp.stack(sums[3:], axis=0) * scale_image, ui[u]

    def batch(b, last):
        places = [8 + 2 * b + i // 2 if i % 2 == 0 else 8 - 2 * b - (i + 1) // 2 for i in range(4)]
        us = [col_peer(d) for d in places]
        parts = [contract(u) for u in us]
        h1, h2, h3 = (jnp.stack([p[0][l] for p in parts], axis=0) for l in range(3))
        back = h1 + box(h2 + box(h3, m) * (1.0 / 9.0), m) * (1.0 / 9.0)
        back = box(back, m) * (2.0 / 27.0)
        image = jnp.stack([p[1] for p in parts], axis=0)
        x = jnp.stack([p[2] for p in parts], axis=0)
        out = merge_lanes(image + back[:, None] * x, m)
        for i, u in enumerate(us):
            if last and i == 3:
                grecv[col] = out[i]
            else:
                gsend[u] = out[i]
                grad_col(places[i], col, u).start()

    loop(0, 3, lambda b: batch(b, False))
    batch(3, True)

    def sent_row(d):
        block_a(d, row, row_peer(d)).wait_send()
        block_b(d, row, row_peer(d)).wait_send()
        image_col(d, col, col_peer(d)).wait_send()
        image_row(d, row, row_peer(d)).wait_send()
        image_tgt(d, row, row_peer(d)).wait_send()
        tile_col(d, col, col_peer(d)).wait_send()
        tile_col_b(d, col, col_peer(d)).wait_send()
        grad_col(d, col, col_peer(d)).wait_send()

    loop(1, GROUP, sent_row)
    loop(1, GROUP, lambda d: grad_col(d, col_peer(d), col).wait_recv())
    total = grecv[0]
    for i in range(1, GROUP):
        total = total + grecv[i]
    for c in range(3):
        for k in range(8):
            grad_out[c, 0:1, k * 128 : (k + 1) * 128] = total[c, k : k + 1, :]


def body(support_views, support_pick, target_views, target_pick, support_labels, target_labels):
    vmem = pl.BlockSpec(memory_space=pltpu.VMEM)
    smem = pl.BlockSpec(memory_space=pltpu.SMEM)
    buf = lambda *shape: pltpu.VMEM(shape, F32)
    grad, label_grad, loss = pl.pallas_call(
        step_kernel,
        name="kip_step",
        out_shape=(
            jax.ShapeDtypeStruct((3, 1, PIX), F32),
            jax.ShapeDtypeStruct((1, CLASSES), F32),
            jax.ShapeDtypeStruct((1, 1), F32),
        ),
        in_specs=[vmem, smem, vmem, smem, vmem, vmem],
        out_specs=(vmem, vmem, vmem),
        scratch_shapes=[
            buf(6, 8, 128),
            buf(GROUP, 6, 8, 128),
            buf(GROUP, 3, 8, 128),
            buf(GROUP, 3, 4, 8, 128),
            buf(GROUP, 6, 4, 8, 128),
            buf(8, 3, 4, 8, 128),
            buf(8, 6, 4, 8, 128),
            buf(3, GROUP, 8, 4, 8, 128),
            buf(3, GROUP, 8, 4, 8, 128),
            buf(8, GROUP, 128),
            buf(GROUP, 8, 128),
            buf(GROUP, 8, 128),
            buf(3, GROUP, 128),
            buf(2, GROUP, 128),
            buf(3, 256, 128),
            buf(2, 256, 128),
            buf(256, 128),
            buf(256, 128),
            buf(32, 128),
            buf(GROUP, 8, 128),
            buf(GROUP, 3, 8, 128),
            buf(GROUP, 3, 8, 128),
        ]
        + [pltpu.SemaphoreType.DMA((GROUP,))] * 16,
        compiler_params=pltpu.CompilerParams(
            collective_id=0, has_side_effects=True, vmem_limit_bytes=56 << 20
        ),
    )(
        jnp.transpose(support_views, (0, 2, 1, 3)),
        support_pick,
        jnp.transpose(target_views, (0, 2, 1, 3)),
        target_pick,
        support_labels,
        target_labels.reshape(1, SUPPORT),
    )
    return jnp.transpose(grad, (1, 0, 2)), label_grad, loss.reshape(())


def solution(mesh):
    both = ("row", "col")
    return jax.shard_map(
        body,
        mesh=mesh,
        in_specs=(
            P(both, None, None, None),
            P(both),
            P(both, None, None, None),
            P(both),
            P(both, None),
            P(),
        ),
        out_specs=(P(both, None, None), P(both, None), P()),
        check_vma=False,
    )
```

```python
import jax
import jax.numpy as jnp
import numpy as np
from jax import lax
from jax.experimental import pallas as pl
from jax.experimental.pallas import tpu as pltpu
from jax.sharding import PartitionSpec as P

PI = float(np.pi)
BIAS = 0.1
RIDGE = 0.1
GROUP = 16
PIX = 1024
SUPPORT = 256
CLASSES = 10
HIGHEST = lax.Precision.HIGHEST
F32 = jnp.float32
BF16 = jnp.bfloat16
ACOS = (
    1.570796251296997,
    -0.21459108591079712,
    0.08883588761091232,
    -0.04919743537902832,
    0.027762912213802338,
    -0.012003393843770027,
    0.0026117200031876564,
)


def inverse_schedule():
    low, high = RIDGE * 0.99, SUPPORT + 2 * RIDGE
    first = 2.0 / (low + high)
    error = (high - low) / (high + low)
    scales = []
    while error > 2e-4:
        scales.append(2.0 / (2.0 - error * error))
        error = error * error / (2.0 - error * error)
    return first, scales


FIRST_SCALE, SCALES = inverse_schedule()
BEFORE = 10
SPLIT = 8
assert GROUP - BEFORE <= 2 * (len(SCALES) - 1)


def make_masks():
    lane = lax.broadcasted_iota(jnp.int32, (8, 128), 1)
    sub = lax.broadcasted_iota(jnp.int32, (8, 128), 0)
    col = lane & 31
    return dict(
        right=(col < 31).astype(F32),
        left=(col > 0).astype(F32),
        below=(sub < 7).astype(F32),
        above=(sub > 0).astype(F32),
        group=lane // 32,
        lane=lane,
    )


def box(x, m):
    h = (
        x
        + m["right"] * pltpu.roll(x, 127, x.ndim - 1)
        + m["left"] * pltpu.roll(x, 1, x.ndim - 1)
    )
    h0, h1, h2, h3 = (h[..., k, :, :] for k in range(4))
    above = pltpu.roll(h3, 1, h3.ndim - 2) * m["above"]
    below = pltpu.roll(h0, 7, h3.ndim - 2) * m["below"]
    a = h0 + h1
    b = h2 + h3
    return jnp.stack([above + a, a + h2, h1 + b, b + below], axis=-3)


def arc(c):
    t = jnp.abs(c)
    w = jnp.maximum(1.0 - t, 1e-30)
    v = 1.0 + t
    q = w * lax.rsqrt(w)
    s = q * (v * lax.rsqrt(v))
    p = jnp.full_like(t, ACOS[-1])
    for a in ACOS[-2::-1]:
        p = p * t + a
    theta = q * p
    return s, jnp.where(c < 0, theta, PI - theta)


def repeat_lanes(x, m):
    rolled = [x] + [pltpu.roll(x, 32 * i, x.ndim - 1) for i in (1, 2, 3)]
    out = []
    for k in range(4):
        y = rolled[0]
        for i in (1, 2, 3):
            y = jnp.where(m["group"] == ((k + i) % 4), rolled[i], y)
        out.append(y)
    return jnp.stack(out, axis=-3)


def pack_lanes(maps, m):
    rolled = [[x if i == 0 else pltpu.roll(x, 32 * i, x.ndim - 1) for i in range(4)] for x in maps]
    out = []
    for k in range(4):
        y = rolled[0][(0 - k) % 4]
        for j in (1, 2, 3):
            y = jnp.where(m["group"] == j, rolled[j][(j - k) % 4], y)
        out.append(y)
    return jnp.stack(out, axis=-3)


def merge_lanes(x, m):
    last = x.ndim - 1
    x = x + pltpu.roll(x, 64, last)
    x = x + pltpu.roll(x, 32, last)
    y = x[..., 0, :, :]
    for k in (1, 2, 3):
        y = jnp.where(m["group"] == k, x[..., k, :, :], y)
    return y


def self_maps(x, m):
    d = box((x[:, 0] * x[:, 0] + x[:, 1] * x[:, 1] + x[:, 2] * x[:, 2]) * (1.0 / 27.0), m) + BIAS
    maps = [d]
    for _ in range(2):
        d = box(d, m) * (1.0 / 9.0) + BIAS
        maps.append(d)
    return maps


def dot3(a, b):
    ah = a.astype(BF16)
    al = (a - ah.astype(F32)).astype(BF16)
    bh = b.astype(BF16)
    bl = (b - bh.astype(F32)).astype(BF16)
    d = lambda p, q: jnp.dot(p, q, preferred_element_type=F32)
    return d(ah, bh) + (d(ah, bl) + d(al, bh))


def dot6(a, b):
    return jnp.dot(a, b, precision=HIGHEST, preferred_element_type=F32)


def dot_nt(a, b):
    return lax.dot_general(
        a, b, (((1,), (1,)), ((), ())), precision=HIGHEST, preferred_element_type=F32
    )


def invert(a, identity, beside):
    x = (SCALES[0] * FIRST_SCALE) * (2.0 * identity - FIRST_SCALE * a)
    count = len(SCALES)
    for i in range(1, count):
        mul = dot6 if i >= count - 1 else dot3
        product = mul(a, x)
        beside(2 * i - 2)
        x = SCALES[i] * mul(x, 2.0 * identity - product)
        beside(2 * i - 1)
    return x


def step_kernel(
    views_ref,
    pick_ref,
    target_views_ref,
    target_pick_ref,
    labels_ref,
    classes_ref,
    grad_out,
    label_out,
    loss_out,
    own,
    vraw,
    uraw,
    ui,
    um,
    vi,
    vm,
    phis,
    sines,
    partial,
    packed,
    packed_b,
    send_a,
    send_b,
    abuf,
    bbuf,
    side1,
    side2,
    wleft,
    wbuf,
    gsend,
    grecv,
    img_row_s,
    img_row_r,
    img_tgt_s,
    img_tgt_r,
    img_col_s,
    img_col_r,
    t1_s,
    t1_r,
    t1b_s,
    t1b_r,
    t2a_s,
    t2a_r,
    t2b_s,
    t2b_r,
    fin_s,
    fin_r,
):
    mesh_row = lax.axis_index("row")
    mesh_col = lax.axis_index("col")
    row = (mesh_col // 4) * 4 + mesh_row // 4
    col = lax.rem(mesh_col, 4) * 4 + lax.rem(mesh_row, 4)
    m = make_masks()

    def device(r, c):
        return (lax.rem(r, 4) * 4 + lax.rem(c, 4), (r // 4) * 4 + c // 4)

    def row_peer(d):
        return lax.rem(row + d, GROUP)

    def col_peer(d):
        return lax.rem(col + d, GROUP)

    def loop(low, high, body):
        def step(d, carry):
            body(d)
            return carry

        lax.fori_loop(low, high, step, 0)

    def far_first(start):
        def pair(k):
            start(8 + k)
            start(7 - k)

        loop(0, 7, pair)
        start(15)

    def remote(src, dst, ssem, rsem, device):
        return pltpu.make_async_remote_copy(
            src_ref=src,
            dst_ref=dst,
            send_sem=ssem,
            recv_sem=rsem,
            device_id=device,
            device_id_type=pl.DeviceIdType.MESH,
        )

    mine = own.at[pl.ds(0, 3)]
    mine_tgt = own.at[pl.ds(3, 3)]

    def image_row(d, slot, peer):
        return remote(
            mine, vraw.at[slot, pl.ds(0, 3)], img_row_s.at[d], img_row_r.at[slot], device(peer, col)
        )

    def image_tgt(d, slot, peer):
        return remote(
            mine_tgt, vraw.at[slot, pl.ds(3, 3)], img_tgt_s.at[d], img_tgt_r.at[slot], device(peer, col)
        )

    def image_col(d, slot, peer):
        return remote(mine, uraw.at[slot], img_col_s.at[d], img_col_r.at[slot], device(row, peer))

    def tile_col(d, slot, peer):
        return remote(packed.at[col], packed.at[slot], t1_s.at[d], t1_r.at[slot], device(row, peer))

    def tile_col_b(d, slot, peer):
        return remote(packed_b.at[col], packed_b.at[slot], t1b_s.at[d], t1b_r.at[slot], device(row, peer))

    def block_a(d, slot, peer):
        return remote(
            send_a, abuf.at[:, pl.ds(slot * GROUP, GROUP)], t2a_s.at[d], t2a_r.at[slot], device(peer, col)
        )

    def block_b(d, slot, peer):
        return remote(
            send_b, bbuf.at[:, pl.ds(slot * GROUP, GROUP)], t2b_s.at[d], t2b_r.at[slot], device(peer, col)
        )

    def grad_col(d, slot, peer):
        return remote(gsend.at[peer], grecv.at[slot], fin_s.at[d], fin_r.at[slot], device(row, peer))

    barrier = pltpu.get_barrier_semaphore()

    def greet(d):
        pl.semaphore_signal(
            barrier, inc=1, device_id=device(row, col_peer(d)), device_id_type=pl.DeviceIdType.MESH
        )
        pl.semaphore_signal(
            barrier, inc=1, device_id=device(row_peer(d), col), device_id_type=pl.DeviceIdType.MESH
        )

    loop(1, GROUP, greet)

    for c in range(3):
        support = views_ref[0, c, pl.ds(pick_ref[0], 1), :]
        target = target_views_ref[0, c, pl.ds(target_pick_ref[0], 1), :]
        for k in range(8):
            own[c, k : k + 1, :] = support[:, k * 128 : (k + 1) * 128]
            own[3 + c, k : k + 1, :] = target[:, k * 128 : (k + 1) * 128]
    pl.semaphore_wait(barrier, 2 * (GROUP - 1))
    far_first(lambda d: image_col(d, col, col_peer(d)).start())
    far_first(lambda d: image_row(d, row, row_peer(d)).start())
    far_first(lambda d: image_tgt(d, row, row_peer(d)).start())
    vraw[row] = own[...]
    uraw[col] = own[0:3]

    def prepare_rows(i):
        us = pl.ds(i * 4, 4)
        x = repeat_lanes(uraw[us], m)
        ui[us] = x
        for l, d in enumerate(self_maps(x, m)):
            r = lax.rsqrt(d)
            um[us, l] = d * r * (1.0 / (9.0 * PI) if l < 2 else 1.0)
            um[us, 3 + l] = r

    def landed_rows(i):
        group = lax.rem(col // 4 + i, 4)

        def landed(k):
            slot = 4 * group + k

            @pl.when(slot != col)
            def _():
                image_col(0, slot, col).wait_recv()

        loop(0, 4, landed)
        prepare_rows(group)

    for i in (0, 1, 3, 2):
        landed_rows(i)


    def prepare_columns(kind):
        vs = slice(4 * kind, 4 * kind + 4)
        x = pack_lanes([vraw[4 * j : 4 * j + 4, 3 * kind : 3 * kind + 3] for j in range(4)], m)
        vi[vs] = x * (1.0 / 27.0)
        for l, d in enumerate(self_maps(x, m)):
            r = lax.rsqrt(d)
            vm[vs, l] = d * r
            vm[vs, 3 + l] = r

    loop(1, GROUP, lambda d: image_row(d, row_peer(d), row).wait_recv())
    prepare_columns(0)

    def forward(kind, low, high):
        vs = slice(4 * kind, 4 * kind + 4)

        def one(u, carry):
            k = box(ui[u, 0] * vi[vs, 0] + ui[u, 1] * vi[vs, 1] + ui[u, 2] * vi[vs, 2], m) + BIAS
            for l in range(3):
                y = k * um[u, 3 + l]
                s, phi = arc(y * vm[vs, 3 + l])
                s = s * vm[vs, l]
                z = (s + phi * y) * um[u, l]
                phis[l, u, vs] = phi
                sines[l, u, vs] = s
                if l < 2:
                    k = box(z, m) + BIAS
            total = jnp.sum(jnp.sum(z, axis=1), axis=1)
            for v in range(4):
                partial[4 * kind + v, pl.ds(u, 1), :] = total[v : v + 1]
            return carry

        lax.fori_loop(low, high, one, 0, unroll=4)

    def pack_tile(kind):
        tile = jnp.zeros((8, 128), F32)
        for half in range(2):
            for j in range(4):
                for v in range(4):
                    part = partial[4 * kind + v, 8 * half : 8 * half + 8, :]
                    total = jnp.sum(jnp.where(m["group"] == j, part, 0.0), axis=1, keepdims=True)
                    tile = jnp.where(m["lane"] == 16 * half + 4 * j + v, total, tile)
        return tile * (1.0 / (PIX * PI))

    def assemble(tiles, block):
        for half in range(2):
            for h in range(2):
                acc = jnp.zeros((8, 128), F32)
                for c in range(8):
                    moved = tiles[8 * h + c]
                    turn = (c - half) % 8
                    if turn:
                        moved = pltpu.roll(moved, 16 * turn, 1)
                    acc = jnp.where(m["lane"] // 16 == c, moved, acc)
                block[h, 8 * half : 8 * half + 8, :] = acc

    def backward(u, carry):
        g = box(phis[2, u], m)
        sines[1, u] = g * sines[1, u]
        g = box(g * phis[1, u], m)
        sines[0, u] = g * sines[0, u]
        phis[0, u] = box(g * phis[0, u], m)
        return carry

    forward(0, 0, GROUP)
    packed[col] = pack_tile(0)
    packed[col, 0:1, 64 : 64 + CLASSES] = labels_ref[...]
    far_first(lambda d: tile_col(d, col, col_peer(d)).start())
    loop(1, GROUP, lambda d: image_tgt(d, row_peer(d), row).wait_recv())
    prepare_columns(1)
    forward(1, 0, SPLIT)
    loop(1, GROUP, lambda d: tile_col(d, col_peer(d), col).wait_recv())
    assemble(packed, send_a)
    for c in range(GROUP):
        send_a[2, c : c + 1, :] = jnp.where(
            m["lane"][0:1] < CLASSES, pltpu.roll(packed[c, 0:1, :], 64, 1), 0.0
        )
    far_first(lambda d: block_a(d, row, row_peer(d)).start())
    abuf[:, pl.ds(row * GROUP, GROUP)] = send_a[...]
    forward(1, SPLIT, GROUP)
    packed_b[col] = pack_tile(1)
    far_first(lambda d: tile_col_b(d, col, col_peer(d)).start())
    lax.fori_loop(0, BEFORE, backward, 0, unroll=2)
    loop(1, GROUP, lambda d: tile_col_b(d, col_peer(d), col).wait_recv())
    assemble(packed_b, send_b)
    far_first(lambda d: block_b(d, row, row_peer(d)).start())
    bbuf[:, pl.ds(row * GROUP, GROUP)] = send_b[...]

    rows = lax.broadcasted_iota(jnp.int32, (256, 256), 0)
    cols = lax.broadcasted_iota(jnp.int32, (256, 256), 1)
    identity = (rows == cols).astype(F32)
    there_col = lax.rem(rows, GROUP)
    there_row = rows // GROUP
    place = (lax.rem(there_col, 4) * 4 + lax.rem(there_row, 4)) * GROUP + (
        (there_col // 4) * 4 + there_row // 4
    )
    permute = (cols == place).astype(BF16)
    class_row = lax.broadcasted_iota(jnp.int32, (16, 256), 0)
    onehot = (classes_ref[...] == class_row).astype(BF16)
    wanted = jnp.dot(onehot, permute, preferred_element_type=F32) - jnp.where(
        class_row < CLASSES, 1.0 / CLASSES, 0.0
    )
    loop(1, GROUP, lambda d: block_a(d, row_peer(d), row).wait_recv())
    ordered = lambda ref, part: jnp.concatenate(
        [ref[part, pl.ds(i, GROUP, stride=GROUP), :] for i in range(GROUP)], axis=0
    )
    kss = jnp.concatenate([ordered(abuf, 0), ordered(abuf, 1)], axis=1)
    trace = jnp.sum(jnp.sum(kss * identity, axis=0, keepdims=True), axis=1, keepdims=True) * (
        1.0 / SUPPORT
    )
    scale = 1.0 / trace
    system = kss * scale + RIDGE * identity

    def beside(i):
        if BEFORE + i < GROUP:
            backward(BEFORE + i, 0)

    inverse = invert(system, identity, beside)

    labels_t = jnp.transpose(ordered(abuf, 2))[0:16]
    alpha_t = dot6(labels_t, inverse)
    alpha_t = (alpha_t + dot6(labels_t - dot6(alpha_t, system), inverse)) * scale

    def sent_early(d):
        image_col(d, col, col_peer(d)).wait_send()
        image_row(d, row, row_peer(d)).wait_send()
        image_tgt(d, row, row_peer(d)).wait_send()
        tile_col(d, col, col_peer(d)).wait_send()
        tile_col_b(d, col, col_peer(d)).wait_send()
        block_a(d, row, row_peer(d)).wait_send()

    loop(1, GROUP, sent_early)
    loop(1, GROUP, lambda d: block_b(d, row_peer(d), row).wait_recv())
    kst = jnp.concatenate([ordered(bbuf, 0), ordered(bbuf, 1)], axis=1)
    error_t = dot6(alpha_t, kst) - wanted
    loss = jnp.sum(jnp.sum(error_t * error_t, axis=0, keepdims=True), axis=1, keepdims=True)
    loss_out[...] = 0.5 * loss
    rhs_t = dot_nt(error_t, kst)
    gamma_t = dot6(rhs_t, inverse)
    gamma_t = (gamma_t + dot6(rhs_t - dot6(gamma_t, system), inverse)) * scale
    inner = jnp.sum(jnp.sum(gamma_t * alpha_t, axis=0, keepdims=True), axis=1, keepdims=True)

    pad = jnp.zeros((80, 256), F32)
    side1[...] = jnp.transpose(jnp.concatenate([alpha_t, gamma_t, error_t, pad], axis=0))
    side2[...] = jnp.transpose(jnp.concatenate([-gamma_t, -alpha_t, alpha_t, pad], axis=0))
    column = side1[pl.ds(col * GROUP, GROUP), :]
    lane16 = lax.broadcasted_iota(jnp.int32, (16, 128), 1)
    for kind in range(2):
        masked = jnp.where((lane16 < 32) == (kind == 0), column, 0.0)
        for j in range(4):
            wleft[8 * j + 4 * kind : 8 * j + 4 * kind + 4, :] = masked[4 * j : 4 * j + 4]
    right = jnp.concatenate(
        [side2[pl.ds(row, GROUP, stride=GROUP), :], jnp.zeros((112, 128), F32)], axis=0
    )
    weights = dot_nt(wleft[...], right)
    lane32 = lax.broadcasted_iota(jnp.int32, (32, 128), 1)
    sub32 = lax.broadcasted_iota(jnp.int32, (32, 128), 0)
    on_diagonal = ((sub32 == 8 * (row // 4) + lax.rem(row, 4)) & (lane32 == col)).astype(F32)
    weights = weights - (2.0 * RIDGE / SUPPORT) * inner * on_diagonal
    own_row = side1[pl.ds(col * GROUP + row, 1), :]
    label_out[...] = own_row[:, 16 : 16 + CLASSES]
    for u in range(GROUP):
        y = weights[0:8, u : u + 1] * jnp.ones((8, 128), F32)
        for j in (1, 2, 3):
            y = jnp.where(m["group"] == j, weights[8 * j : 8 * j + 8, u : u + 1], y)
        wbuf[u] = y

    step9 = 1.0 / (9.0 * PI)
    each = 1.0 / (2.0 * PI * PIX)
    scale_image = 27.0 * step9**3 / (3.0 * PIX)

    def contract(u):
        sums = None
        for v in range(8):
            w = jnp.broadcast_to(wbuf[u, v : v + 1, :], (8, 128))
            g = w * phis[0, u, v]
            terms = [w * sines[l, u, v] for l in range(3)] + [g * vi[v, c] for c in range(3)]
            sums = terms if sums is None else [a + b for a, b in zip(sums, terms)]
        h = [sums[l] * um[u, 3 + l] * (each * step9 ** (2 - l)) for l in range(3)]
        return h, jnp.stack(sums[3:], axis=0) * scale_image, ui[u]

    def batch(b, last):
        places = [8 + 2 * b + i // 2 if i % 2 == 0 else 8 - 2 * b - (i + 1) // 2 for i in range(4)]
        us = [col_peer(d) for d in places]
        parts = [contract(u) for u in us]
        h1, h2, h3 = (jnp.stack([p[0][l] for p in parts], axis=0) for l in range(3))
        back = h1 + box(h2 + box(h3, m) * (1.0 / 9.0), m) * (1.0 / 9.0)
        back = box(back, m) * (2.0 / 27.0)
        image = jnp.stack([p[1] for p in parts], axis=0)
        x = jnp.stack([p[2] for p in parts], axis=0)
        out = merge_lanes(image + back[:, None] * x, m)
        for i, u in enumerate(us):
            if last and i == 3:
                grecv[col] = out[i]
            else:
                gsend[u] = out[i]
                grad_col(places[i], col, u).start()

    loop(0, 3, lambda b: batch(b, False))
    batch(3, True)

    def sent_late(d):
        block_b(d, row, row_peer(d)).wait_send()
        grad_col(d, col, col_peer(d)).wait_send()

    loop(1, GROUP, sent_late)
    loop(1, GROUP, lambda d: grad_col(d, col_peer(d), col).wait_recv())
    total = grecv[0]
    for i in range(1, GROUP):
        total = total + grecv[i]
    for c in range(3):
        for k in range(8):
            grad_out[c, 0:1, k * 128 : (k + 1) * 128] = total[c, k : k + 1, :]


def body(support_views, support_pick, target_views, target_pick, support_labels, target_labels):
    vmem = pl.BlockSpec(memory_space=pltpu.VMEM)
    smem = pl.BlockSpec(memory_space=pltpu.SMEM)
    buf = lambda *shape: pltpu.VMEM(shape, F32)
    grad, label_grad, loss = pl.pallas_call(
        step_kernel,
        name="kip_step",
        out_shape=(
            jax.ShapeDtypeStruct((3, 1, PIX), F32),
            jax.ShapeDtypeStruct((1, CLASSES), F32),
            jax.ShapeDtypeStruct((1, 1), F32),
        ),
        in_specs=[vmem, smem, vmem, smem, vmem, vmem],
        out_specs=(vmem, vmem, vmem),
        scratch_shapes=[
            buf(6, 8, 128),
            buf(GROUP, 6, 8, 128),
            buf(GROUP, 3, 8, 128),
            buf(GROUP, 3, 4, 8, 128),
            buf(GROUP, 6, 4, 8, 128),
            buf(8, 3, 4, 8, 128),
            buf(8, 6, 4, 8, 128),
            buf(3, GROUP, 8, 4, 8, 128),
            buf(3, GROUP, 8, 4, 8, 128),
            buf(8, GROUP, 128),
            buf(GROUP, 8, 128),
            buf(GROUP, 8, 128),
            buf(3, GROUP, 128),
            buf(2, GROUP, 128),
            buf(3, 256, 128),
            buf(2, 256, 128),
            buf(256, 128),
            buf(256, 128),
            buf(32, 128),
            buf(GROUP, 8, 128),
            buf(GROUP, 3, 8, 128),
            buf(GROUP, 3, 8, 128),
        ]
        + [pltpu.SemaphoreType.DMA((GROUP,))] * 16,
        compiler_params=pltpu.CompilerParams(
            collective_id=0, has_side_effects=True, vmem_limit_bytes=56 << 20
        ),
    )(
        jnp.transpose(support_views, (0, 2, 1, 3)),
        support_pick,
        jnp.transpose(target_views, (0, 2, 1, 3)),
        target_pick,
        support_labels,
        target_labels.reshape(1, SUPPORT),
    )
    return jnp.transpose(grad, (1, 0, 2)), label_grad, loss.reshape(())


def solution(mesh):
    both = ("row", "col")
    return jax.shard_map(
        body,
        mesh=mesh,
        in_specs=(
            P(both, None, None, None),
            P(both),
            P(both, None, None, None),
            P(both),
            P(both, None),
            P(),
        ),
        out_specs=(P(both, None, None), P(both, None), P()),
        check_vma=False,
    )
```
